256 devices in a mesh: row: 16 (over x, y_hi, core), col: 16 (over z, y_lo).
Axes of the slice: x: 4, y: 4 (y_hi: 2, y_lo: 2; y = y_hi * 2 + y_lo), z: 8, core: 2. Of those that a mesh axis runs over, the one named last changes fastest.
Arguments:
- panel_cols: bfloat16 [48, 4096, 512], P('col', 'row'), may hold values from -6 to 6
- inverses: bfloat16 [2, 256, 256], replicated, as said below
- trailing: bfloat16 [48, 4096, 4096], P(None, 'row', 'col'), may hold values from -6 to 6
Outputs:
- updated: bfloat16 [48, 4096, 4096], P(None, 'row', 'col')
The draws below stay inside these ranges and needn't reach their ends.
Inputs may be any that keep to these rules, and one draw needn't show every extreme that they name: `inverses`: each of the two 256 x 256 matrices is lower triangular with a positive diagonal.
All inputs are finite; a program needn't handle non-finite values.
Results may differ from the reference program's by a relative error of at most 0.0063.
Values may be sent and summed in bfloat16 or wider, within the bound.
A program may use at most 128 MiB of HBM per device.

```python
import jax
import jax.numpy as jnp
from jax import lax

TILE = 256
TR_DEV = 48
TRAIL = 4096
N_ROW = 16
N_COL = 16


def draw_inverses(key, part):
    first_key, second_key = jax.random.split(jax.random.fold_in(key, 7))
    below = (jnp.arange(TILE)[:, None] > jnp.arange(TILE)[None, :]).astype(jnp.float32)
    identity = jnp.eye(TILE, dtype=jnp.float32)
    lower_part = jax.random.normal(first_key, (2, TILE, TILE), jnp.float32) / 64.0
    diag_vals = jax.random.uniform(second_key, (2, TILE, 1), jnp.float32, 0.2, 0.35)
    matrix = lower_part * below[None] + diag_vals * identity[None]
    return matrix.astype(jnp.bfloat16)


def shard_levels(own_key, extent, cuts, smallest, largest):
    loudness = 1.0
    for position, shards_of in cuts:
        steps = jax.random.uniform(jax.random.fold_in(jax.random.fold_in(own_key, 6), position), (shards_of,), jnp.float32, smallest / len(cuts), largest / len(cuts))
        loudness = loudness * jnp.repeat(jnp.exp(steps), extent[position] // shards_of).reshape((-1,) + (1,) * (len(extent) - 1 - position))
    return loudness


def noise(own_key, extent, width, limit, cuts=(), kind=jnp.bfloat16):
    gain = shard_levels(own_key, extent, cuts, -0.22, 0.18) if cuts else 1.0
    values = jax.random.normal(own_key, extent, jnp.float32) * width * gain
    return jnp.minimum(jnp.maximum(values, -limit), limit).astype(kind)


def setup_inputs(seed: int = 0) -> dict:
    arg_keys = jax.random.split(jax.random.key(seed), 4)
    panel_cols = noise(arg_keys[0], (TR_DEV, N_ROW * TILE, 2 * TILE), 1.0, 6.0, ((0, 16), (1, 16)))
    inverses = draw_inverses(jax.random.fold_in(arg_keys[3], 71), 0)
    trailing = noise(arg_keys[2], (TR_DEV, N_ROW * TILE, TRAIL), 1.0, 6.0, ((1, 16), (2, 16)))
    return {"panel_cols": panel_cols, "inverses": inverses, "trailing": trailing}


def reference(panel_cols, inverses, trailing):
    flat_panel = panel_cols.reshape(-1, 2 * TILE)
    left_factor = jnp.dot(flat_panel[:, :TILE], inverses[0].T, preferred_element_type=jnp.float32).astype(jnp.bfloat16)
    couple_tile = left_factor[TILE:2 * TILE]
    reduced = (flat_panel[:, TILE:].astype(jnp.float32) - jnp.dot(left_factor, couple_tile.T, preferred_element_type=jnp.float32)).astype(jnp.bfloat16)
    right_factor = jnp.dot(reduced, inverses[1].T, preferred_element_type=jnp.float32).astype(jnp.bfloat16)
    factored = jnp.concatenate([left_factor, right_factor], axis=1)
    key_rows = factored[2 * TILE:(N_COL + 2) * TILE].reshape(N_COL, TILE, 2 * TILE)
    columns = jnp.moveaxis(trailing.reshape(-1, N_COL, TILE), 1, 0)

    def update_column(column_pair):
        column_block, key_tile = column_pair
        return (column_block.astype(jnp.float32) - jnp.dot(factored, key_tile.T, preferred_element_type=jnp.float32)).astype(jnp.bfloat16)

    result = lax.map(update_column, (columns, key_rows))
    return jnp.moveaxis(result, 0, 1).reshape(trailing.shape)
```

```python
import functools

import jax
import jax.numpy as jnp
from jax import lax
from jax.experimental import pallas as pl
from jax.experimental.pallas import tpu as pltpu
from jax.sharding import PartitionSpec as P

MESH = pl.DeviceIdType.MESH
TILE = 256
SHARED = 128
PIECE = 16


def times_transposed(left, right):
    return lax.dot_general(left, right, (((1,), (1,)), ((), ())), preferred_element_type=jnp.float32)


def kernel(
    panel, inverses, trailing, updated,
    own, mate, shared, sums_in, sums_out, window, pieces, couple, keys,
    ring_send, ring_recv, mate_send, mate_recv, sum_send, sum_recv,
    load_sem, piece_sem, spread_send, spread_recv, out_sem,
):
    row, col = lax.axis_index("row"), lax.axis_index("col")
    z, y = col // 2, lax.rem(col, 2)
    chip, core = row // 2, lax.rem(row, 2)
    my_piece = core * PIECE + chip * 2 + y
    mate_dev = (row, col + 1 - 2 * y)
    ring_dev = ((row, lax.rem(col + 2, 16)), (row, lax.rem(col + 14, 16)))
    plain = TILE - SHARED

    load_own = pltpu.make_async_copy(panel, own.at[z], load_sem.at[0])
    load_window = pltpu.make_async_copy(trailing, window, load_sem.at[1])
    load_own.start()
    load_window.start()

    def plane_device(q, plane):
        at = lax.rem(q, PIECE)
        return ((at // 2) * 2 + q // PIECE, plane * 2 + lax.rem(at, 2))

    key_plane = lax.rem(row + 14, 16) // 2
    key_source = lax.rem(z * 2 + core + 2, 16)
    is_source = col == 0
    is_couple = jnp.logical_and(is_source, row == 1)

    barrier = pltpu.get_barrier_semaphore()

    def greet(dev):
        pl.semaphore_signal(barrier, inc=1, device_id=dev, device_id_type=MESH)

    def greet_plane(q, carry):
        @pl.when(q != my_piece)
        def _():
            greet(plane_device(q, z))

        return carry

    lax.fori_loop(0, 2 * PIECE, greet_plane, 0)
    greet(ring_dev[0])
    greet(ring_dev[1])

    @pl.when(z != 0)
    def _():
        greet((key_source, 0))
        greet((row, y))

    from_keys = jnp.where(jnp.logical_and(is_source, key_plane != 0), 16, 0)
    from_couple = jnp.where(z == 0, 7, 0)
    pl.semaphore_wait(barrier, 33 + from_keys + from_couple)

    load_own.wait()

    def is_shared(unit):
        return isinstance(unit, int) and unit == 3

    def ring_ref(d, s, unit):
        place = lax.rem(z + 8 - s, 8) if d == 0 else lax.rem(z + s, 8)
        return shared.at[place] if is_shared(unit) else own.at[place, unit]

    def ring_copy(d, s, unit, half):
        ref = ring_ref(d, s, unit)
        if half:
            rows = (SHARED if is_shared(unit) else TILE) // 2
            ref = ref.at[pl.ds(d * rows, rows)]
        return pltpu.make_async_remote_copy(
            ref, ref, ring_send.at[d, s, unit], ring_recv.at[d, s, unit],
            device_id=ring_dev[d], device_id_type=MESH,
        )

    def arrived(d, s, unit, half=False):
        ref = ring_ref(d, s, unit)
        if half:
            rows = (SHARED if is_shared(unit) else TILE) // 2
            ref = ref.at[pl.ds(d * rows, rows)]
        pltpu.make_async_remote_copy(
            ref, ref, ring_send.at[d, s - 1, unit], ring_recv.at[d, s - 1, unit],
            device_id=ring_dev[d], device_id_type=MESH,
        ).wait_recv()

    def mate_copy(unit):
        if unit == 3:
            ref, dst = own.at[z, 2, pl.ds(plain, SHARED)], shared.at[z]
        elif unit == 2:
            ref, dst = own.at[z, 2, pl.ds(0, plain)], mate.at[2, pl.ds(0, plain)]
        else:
            ref, dst = own.at[z, unit], mate.at[unit]
        return pltpu.make_async_remote_copy(
            ref, dst, mate_send.at[unit], mate_recv.at[unit], device_id=mate_dev, device_id_type=MESH
        )

    key_tile = jnp.where(row < 2, 1, 0)

    @pl.when(is_couple)
    def _():
        def send(q, carry):
            src = own.at[0, 0, pl.ds(lax.rem(q, PIECE) * 16, 16), pl.ds((q // PIECE) * 128, 128)]
            dst = pieces.at[q, :, pl.ds(512, 128)]

            @pl.when(q != my_piece)
            def _():
                pltpu.make_async_remote_copy(
                    src, dst, piece_sem.at[2], piece_sem.at[3], device_id=plane_device(q, 0), device_id_type=MESH
                ).start()

            @pl.when(q == my_piece)
            def _():
                pltpu.make_async_copy(src, dst, piece_sem.at[3]).start()

            return carry

        lax.fori_loop(0, 2 * PIECE, send, 0)

    @pl.when(is_source)
    def _():
        def send(p, carry):
            q = core * PIECE + p
            src = own.at[0, key_tile, pl.ds(p * 16, 16)]
            dst = pieces.at[q, :, pl.ds(0, 512)]
            itself = jnp.logical_and(key_plane == 0, q == my_piece)

            @pl.when(jnp.logical_not(itself))
            def _():
                pltpu.make_async_remote_copy(
                    src, dst, piece_sem.at[0], piece_sem.at[1], device_id=plane_device(q, key_plane),
                    device_id_type=MESH,
                ).start()

            @pl.when(itself)
            def _():
                pltpu.make_async_copy(src, dst, piece_sem.at[1]).start()

            return carry

        lax.fori_loop(0, PIECE, send, 0)

    for unit in (3, 0, 1, 2):
        mate_copy(unit).start()
        if unit != 3:
            for d in (0, 1):
                ring_copy(d, 0, unit, False).start()

    mine = pieces.at[my_piece]
    pltpu.make_async_copy(mine.at[:, pl.ds(512, 128)], mine.at[:, pl.ds(512, 128)], piece_sem.at[3]).wait()

    @pl.when(z == 0)
    def _():
        def send(i, carry):
            ref = mine.at[:, pl.ds(512, 128)]
            pltpu.make_async_remote_copy(
                ref, ref, piece_sem.at[4], piece_sem.at[3], device_id=(row, (i + 1) * 2 + y), device_id_type=MESH
            ).start()
            return carry

        lax.fori_loop(0, 7, send, 0)

    mate_copy(3).wait_recv()
    for d in (0, 1):
        ring_copy(d, 0, 3, False).start()

    pltpu.make_async_copy(mine.at[:, pl.ds(0, 512)], mine.at[:, pl.ds(0, 512)], piece_sem.at[1]).wait()

    def spread(q, carry):
        @pl.when(q != my_piece)
        def _():
            pltpu.make_async_remote_copy(
                mine, mine, spread_send, spread_recv, device_id=plane_device(q, z), device_id_type=MESH
            ).start()

        return carry

    lax.fori_loop(0, 2 * PIECE, spread, 0)

    for unit in (0, 1, 2):
        for d in (0, 1):
            arrived(d, 1, unit)
            ring_copy(d, 1, unit, False).start()

    peers = 2 * PIECE - 1
    pltpu.make_async_copy(pieces.at[pl.ds(0, peers)], pieces.at[pl.ds(0, peers)], spread_recv).wait()

    for part in (0, 1):
        raw = pieces[part * PIECE:(part + 1) * PIECE, :, 512:640].reshape(TILE, 128)
        keys[0, :, part * 128:(part + 1) * 128] = raw
    couple[...] = times_transposed(keys[0, :, 0:TILE], inverses[0]).astype(jnp.bfloat16)

    def factor(raw):
        left = times_transposed(raw[:, 0:TILE], inverses[0]).astype(jnp.bfloat16)
        reduced = (raw[:, TILE:].astype(jnp.float32) - times_transposed(left, couple[...])).astype(jnp.bfloat16)
        right = times_transposed(reduced, inverses[1]).astype(jnp.bfloat16)
        return left, right

    def product(factors, which):
        left, right = factors
        return times_transposed(left, keys[which, :, 0:TILE]) + times_transposed(right, keys[which, :, TILE:])

    for which in (0, 1):
        parity = y if which == 0 else 1 - y
        raw = pieces[pl.ds(parity * PIECE, PIECE), :, 0:512].reshape(TILE, 2 * TILE)
        left, right = factor(raw)
        keys[which, :, 0:TILE] = left
        keys[which, :, TILE:] = right

    load_window.wait()

    def subtract(tile, start, rows, amount):
        at = (tile, pl.ds(start, rows))
        window[at] = (window[at].astype(jnp.float32) - amount.astype(jnp.float32)).astype(jnp.bfloat16)
        pltpu.make_async_copy(window.at[at], updated.at[at], out_sem).start()

    def own_tile(place, unit):
        return (place * 2 + y) * 3 + unit

    def mate_tile(place, unit):
        return (place * 2 + 1 - y) * 3 + unit

    def local_tile(unit, carry):
        subtract(own_tile(z, unit), 0, TILE, product(factor(own[z, unit]), 0))
        return carry

    lax.fori_loop(0, 3, local_tile, 0)
    for unit in (0, 1):
        mate_copy(unit).wait_recv()
        subtract(mate_tile(z, unit), 0, TILE, product(factor(mate[unit]), 0))
    mate_copy(2).wait_recv()
    subtract(mate_tile(z, 2), 0, plain, product(factor(mate[2, 0:plain]), 0))
    subtract(mate_tile(z, 2), plain, SHARED, product(factor(shared[z]), 0))

    def place_of(d, s):
        return lax.rem(z + jnp.where(d == 0, 8 - s, s), 8)

    def sum_copy(place, unit, rows):
        return pltpu.make_async_remote_copy(
            sums_out.at[place, unit, pl.ds(0, rows)], sums_in.at[place, unit, pl.ds(0, rows)],
            sum_send.at[place, unit], sum_recv.at[place, unit], device_id=mate_dev, device_id_type=MESH,
        )

    def column_tile(place, unit):
        factors = factor(own[place, unit])
        sums_out[place, unit] = product(factors, 1).astype(jnp.bfloat16)

        @pl.when(unit != 2)
        def _():
            sum_copy(place, unit, TILE).start()

        @pl.when(unit == 2)
        def _():
            sum_copy(place, unit, plain).start()

        subtract(own_tile(place, unit), 0, TILE, product(factors, 0))

    def finish(place, unit):
        @pl.when(unit != 2)
        def _():
            sum_copy(place, unit, TILE).wait_recv()
            subtract(mate_tile(place, unit), 0, TILE, sums_in[place, unit])

        @pl.when(unit == 2)
        def _():
            sum_copy(place, unit, plain).wait_recv()
            subtract(mate_tile(place, unit), 0, plain, sums_in[place, unit, 0:plain])

    def shared_tile(place):
        subtract(mate_tile(place, 2), plain, SHARED, product(factor(shared[place]), 0))

    def pair(i, compute):
        s, unit = i // 3 + 1, lax.rem(i, 3)

        def one(d, carry):
            compute(place_of(d, s), unit)
            return carry

        lax.fori_loop(0, 2, one, 0)

    def visit(i, carry):
        s, unit = i // 3 + 1, lax.rem(i, 3)

        @pl.when(s > 1)
        def _():
            for d in (0, 1):
                arrived(d, s, unit)

                @pl.when(s == 2)
                def _():
                    ring_copy(d, s, unit, False).start()

                @pl.when(s == 3)
                def _():
                    ring_copy(d, s, unit, True).start()

        pair(i, column_tile)

        @pl.when(i > 0)
        def _():
            pair(i - 1, finish)

        @pl.when(unit == 2)
        def _():
            for d in (0, 1):
                arrived(d, s, 3)

                @pl.when(s < 3)
                def _():
                    ring_copy(d, s, 3, False).start()

                @pl.when(s == 3)
                def _():
                    ring_copy(d, s, 3, True).start()

            def one(d, carry):
                shared_tile(place_of(d, s))
                return carry

            lax.fori_loop(0, 2, one, 0)

        return carry

    lax.fori_loop(0, 9, visit, 0)

    far = lax.rem(z + 4, 8)

    def last(unit, carry):
        for d in (0, 1):
            arrived(d, 4, unit, True)
        column_tile(far, unit)

        @pl.when(unit == 0)
        def _():
            pair(8, finish)

        @pl.when(unit > 0)
        def _():
            finish(far, unit - 1)

        return carry

    lax.fori_loop(0, 3, last, 0)
    for d in (0, 1):
        arrived(d, 4, 3, True)
    shared_tile(far)
    finish(far, 2)

    for unit in range(4):
        mate_copy(unit).wait_send()
        for d in (0, 1):
            for s in range(4):
                ring_copy(d, s, unit, s == 3).wait_send()

    def drain(i, carry):
        place = lax.rem(z + i, 8)
        for unit in range(3):
            sum_copy(place, unit, plain if unit == 2 else TILE).wait_send()
        return carry

    lax.fori_loop(1, 8, drain, 0)
    pltpu.make_async_copy(pieces.at[pl.ds(0, peers)], pieces.at[pl.ds(0, peers)], spread_send).wait()

    @pl.when(z == 0)
    def _():
        ref = pieces.at[pl.ds(0, 7), :, pl.ds(512, 128)]
        pltpu.make_async_copy(ref, ref, piece_sem.at[4]).wait()

    @pl.when(is_source)
    def _():
        @pl.when(key_plane == 0)
        def _():
            ref = own.at[0, 0, pl.ds(0, 240)]
            pltpu.make_async_copy(ref, ref, piece_sem.at[0]).wait()

        @pl.when(key_plane != 0)
        def _():
            ref = own.at[0, 0]
            pltpu.make_async_copy(ref, ref, piece_sem.at[0]).wait()

    @pl.when(is_couple)
    def _():
        ref = pieces.at[pl.ds(0, peers), :, pl.ds(512, 128)]
        pltpu.make_async_copy(ref, ref, piece_sem.at[2]).wait()

    pltpu.make_async_copy(window, updated, out_sem).wait()


def shards(panel_cols, inverses, trailing):
    bf16 = jnp.bfloat16
    return pl.pallas_call(
        kernel,
        out_shape=jax.ShapeDtypeStruct(trailing.shape, bf16),
        in_specs=[
            pl.BlockSpec(memory_space=pl.ANY),
            pl.BlockSpec(memory_space=pltpu.VMEM),
            pl.BlockSpec(memory_space=pl.ANY),
        ],
        out_specs=pl.BlockSpec(memory_space=pl.ANY),
        scratch_shapes=[
            pltpu.VMEM((8, 3, TILE, 2 * TILE), bf16),
            pltpu.VMEM((3, TILE, 2 * TILE), bf16),
            pltpu.VMEM((8, SHARED, 2 * TILE), bf16),
            pltpu.VMEM((8, 3, TILE, TILE), bf16),
            pltpu.VMEM((8, 3, TILE, TILE), bf16),
            pltpu.VMEM((48, TILE, TILE), bf16),
            pltpu.VMEM((2 * PIECE, 16, 640), bf16),
            pltpu.VMEM((TILE, TILE), bf16),
            pltpu.VMEM((2, TILE, 2 * TILE), bf16),
            pltpu.SemaphoreType.DMA((2, 4, 4)),
            pltpu.SemaphoreType.DMA((2, 4, 4)),
            pltpu.SemaphoreType.DMA((4,)),
            pltpu.SemaphoreType.DMA((4,)),
            pltpu.SemaphoreType.DMA((8, 3)),
            pltpu.SemaphoreType.DMA((8, 3)),
            pltpu.SemaphoreType.DMA((2,)),
            pltpu.SemaphoreType.DMA((5,)),
            pltpu.SemaphoreType.DMA,
            pltpu.SemaphoreType.DMA,
            pltpu.SemaphoreType.DMA,
        ],
        compiler_params=pltpu.CompilerParams(
            collective_id=0, has_side_effects=True, vmem_limit_bytes=56 << 20
        ),
        name="panel_update",
    )(panel_cols, inverses, trailing)


def solution(mesh):
    in_specs = (P("col", "row", None), P(), P(None, "row", "col"))
    out_specs = P(None, "row", "col")
    return jax.shard_map(shards, mesh=mesh, in_specs=in_specs, out_specs=out_specs, check_vma=False)
```

```python
import functools

import jax
import jax.numpy as jnp
from jax import lax
from jax.experimental import pallas as pl
from jax.experimental.pallas import tpu as pltpu
from jax.sharding import PartitionSpec as P

MESH = pl.DeviceIdType.MESH
TILE = 256
SHARED = 128
PIECE = 16


def times_transposed(left, right):
    return lax.dot_general(left, right, (((1,), (1,)), ((), ())), preferred_element_type=jnp.float32)


def kernel(
    panel, inverses, trailing, window,
    own, mate, shared, sums_in, sums_out, stage, couple_piece, pieces, couple, keys,
    ring_send, ring_recv, mate_send, mate_recv, sum_send, sum_recv,
    load_sem, piece_sem, spread_send, spread_recv,
):
    row, col = lax.axis_index("row"), lax.axis_index("col")
    z, y = col // 2, lax.rem(col, 2)
    chip, core = row // 2, lax.rem(row, 2)
    my_piece = core * PIECE + chip * 2 + y
    mate_dev = (row, col + 1 - 2 * y)
    ring_dev = ((row, lax.rem(col + 2, 16)), (row, lax.rem(col + 14, 16)))
    plain = TILE - SHARED

    load_own = pltpu.make_async_copy(panel, own.at[z], load_sem.at[0])
    load_window = pltpu.make_async_copy(trailing, window, load_sem.at[1])
    load_own.start()
    load_window.start()

    def plane_device(q, plane):
        at = lax.rem(q, PIECE)
        return ((at // 2) * 2 + q // PIECE, plane * 2 + lax.rem(at, 2))

    key_plane = lax.rem(row + 14, 16) // 2
    is_source = col == 0
    is_couple = jnp.logical_and(is_source, row == 1)

    barrier = pltpu.get_barrier_semaphore()

    def greet(dev):
        pl.semaphore_signal(barrier, inc=1, device_id=dev, device_id_type=MESH)

    def greet_plane(q, carry):
        @pl.when(q != my_piece)
        def _():
            greet(plane_device(q, z))

        return carry

    lax.fori_loop(0, 2 * PIECE, greet_plane, 0)
    greet(ring_dev[0])
    greet(ring_dev[1])

    @pl.when(z != 0)
    def _():
        greet((row, y))

    pl.semaphore_wait(barrier, 33 + jnp.where(z == 0, 7, 0))

    load_own.wait()

    def is_shared(unit):
        return isinstance(unit, int) and unit == 3

    def ring_ref(d, s, unit):
        place = lax.rem(z + 8 - s, 8) if d == 0 else lax.rem(z + s, 8)
        return shared.at[place] if is_shared(unit) else own.at[place, unit]

    def ring_copy(d, s, unit, half):
        ref = ring_ref(d, s, unit)
        if half:
            rows = (SHARED if is_shared(unit) else TILE) // 2
            ref = ref.at[pl.ds(d * rows, rows)]
        return pltpu.make_async_remote_copy(
            ref, ref, ring_send.at[d, s, unit], ring_recv.at[d, s, unit],
            device_id=ring_dev[d], device_id_type=MESH,
        )

    def arrived(d, s, unit, half=False):
        ref = ring_ref(d, s, unit)
        if half:
            rows = (SHARED if is_shared(unit) else TILE) // 2
            ref = ref.at[pl.ds(d * rows, rows)]
        pltpu.make_async_remote_copy(
            ref, ref, ring_send.at[d, s - 1, unit], ring_recv.at[d, s - 1, unit],
            device_id=ring_dev[d], device_id_type=MESH,
        ).wait_recv()

    def mate_copy(unit):
        if unit == 3:
            ref, dst = own.at[z, 2, pl.ds(plain, SHARED)], shared.at[z]
        elif unit == 2:
            ref, dst = own.at[z, 2, pl.ds(0, plain)], mate.at[2, pl.ds(0, plain)]
        else:
            ref, dst = own.at[z, unit], mate.at[unit]
        return pltpu.make_async_remote_copy(
            ref, dst, mate_send.at[unit], mate_recv.at[unit], device_id=mate_dev, device_id_type=MESH
        )

    key_tile = jnp.where(row < 2, 1, 0)

    @pl.when(is_couple)
    def _():
        def send(q, carry):
            src = own.at[0, 0, pl.ds(lax.rem(q, PIECE) * 16, 16), pl.ds((q // PIECE) * 128, 128)]

            @pl.when(q != my_piece)
            def _():
                pltpu.make_async_remote_copy(
                    src, couple_piece, piece_sem.at[2], piece_sem.at[3], device_id=plane_device(q, 0),
                    device_id_type=MESH,
                ).start()

            @pl.when(q == my_piece)
            def _():
                pltpu.make_async_copy(src, couple_piece, piece_sem.at[3]).start()

            return carry

        lax.fori_loop(0, 2 * PIECE, send, 0)

    @pl.when(is_source)
    def _():
        def send(p, carry):
            q = core * PIECE + p
            src = own.at[0, key_tile, pl.ds(p * 16, 16)]
            dst = stage.at[key_plane, :, pl.ds(0, 512)]

            @pl.when(q != my_piece)
            def _():
                pltpu.make_async_remote_copy(
                    src, dst, piece_sem.at[0], piece_sem.at[1], device_id=plane_device(q, 0), device_id_type=MESH
                ).start()

            @pl.when(q == my_piece)
            def _():
                pltpu.make_async_copy(src, dst, piece_sem.at[1]).start()

            return carry

        lax.fori_loop(0, PIECE, send, 0)

    for unit in (3, 0, 1, 2):
        mate_copy(unit).start()
        if unit != 3:
            for d in (0, 1):
                ring_copy(d, 0, unit, False).start()

    mine = pieces.at[my_piece]

    @pl.when(z == 0)
    def _():
        staged = stage.at[:, :, pl.ds(0, 512)]
        pltpu.make_async_copy(couple_piece, couple_piece, piece_sem.at[3]).wait()
        pltpu.make_async_copy(staged, staged, piece_sem.at[1]).wait()
        for plane in range(8):
            stage[plane, :, 512:640] = couple_piece[...]

        def send(plane, carry):
            pltpu.make_async_remote_copy(
                stage.at[plane], mine, piece_sem.at[4], piece_sem.at[5], device_id=(row, plane * 2 + y),
                device_id_type=MESH,
            ).start()
            return carry

        lax.fori_loop(1, 8, send, 0)
        pieces[my_piece] = stage[0]

    mate_copy(3).wait_recv()
    for d in (0, 1):
        ring_copy(d, 0, 3, False).start()

    @pl.when(z != 0)
    def _():
        pltpu.make_async_copy(mine, mine, piece_sem.at[5]).wait()

    def spread(q, carry):
        @pl.when(q != my_piece)
        def _():
            pltpu.make_async_remote_copy(
                mine, mine, spread_send, spread_recv, device_id=plane_device(q, z), device_id_type=MESH
            ).start()

        return carry

    lax.fori_loop(0, 2 * PIECE, spread, 0)

    for unit in (0, 1, 2):
        for d in (0, 1):
            arrived(d, 1, unit)
            ring_copy(d, 1, unit, False).start()

    peers = 2 * PIECE - 1
    pltpu.make_async_copy(pieces.at[pl.ds(0, peers)], pieces.at[pl.ds(0, peers)], spread_recv).wait()

    for part in (0, 1):
        raw = pieces[part * PIECE:(part + 1) * PIECE, :, 512:640].reshape(TILE, 128)
        keys[0, :, part * 128:(part + 1) * 128] = raw
    couple[...] = times_transposed(keys[0, :, 0:TILE], inverses[0]).astype(jnp.bfloat16)

    def factor(raw):
        left = times_transposed(raw[:, 0:TILE], inverses[0]).astype(jnp.bfloat16)
        reduced = (raw[:, TILE:].astype(jnp.float32) - times_transposed(left, couple[...])).astype(jnp.bfloat16)
        right = times_transposed(reduced, inverses[1]).astype(jnp.bfloat16)
        return left, right

    def product(factors, which):
        left, right = factors
        return times_transposed(left, keys[which, :, 0:TILE]) + times_transposed(right, keys[which, :, TILE:])

    for which in (0, 1):
        parity = y if which == 0 else 1 - y
        raw = pieces[pl.ds(parity * PIECE, PIECE), :, 0:512].reshape(TILE, 2 * TILE)
        left, right = factor(raw)
        keys[which, :, 0:TILE] = left
        keys[which, :, TILE:] = right

    load_window.wait()

    def subtract(tile, start, rows, amount):
        at = (tile, pl.ds(start, rows))
        window[at] = (window[at].astype(jnp.float32) - amount.astype(jnp.float32)).astype(jnp.bfloat16)

    def own_tile(place, unit):
        return (place * 2 + y) * 3 + unit

    def mate_tile(place, unit):
        return (place * 2 + 1 - y) * 3 + unit

    for unit in (0, 1, 2):
        mate_copy(unit).wait_recv()
    mate[2, plain:TILE] = shared[z]

    def local_tile(unit):
        subtract(own_tile(z, unit), 0, TILE, product(factor(own[z, unit]), 0))
        subtract(mate_tile(z, unit), 0, TILE, product(factor(mate[unit]), 0))

    def place_of(d, s):
        return lax.rem(z + jnp.where(d == 0, 8 - s, s), 8)

    def sum_copy(place, unit, rows):
        return pltpu.make_async_remote_copy(
            sums_out.at[place, unit, pl.ds(0, rows)], sums_in.at[place, unit, pl.ds(0, rows)],
            sum_send.at[place, unit], sum_recv.at[place, unit], device_id=mate_dev, device_id_type=MESH,
        )

    def column_tile(place, unit):
        factors = factor(own[place, unit])
        sums_out[place, unit] = product(factors, 1).astype(jnp.bfloat16)

        @pl.when(unit != 2)
        def _():
            sum_copy(place, unit, TILE).start()

        @pl.when(unit == 2)
        def _():
            sum_copy(place, unit, plain).start()

        subtract(own_tile(place, unit), 0, TILE, product(factors, 0))

    def finish(place, unit):
        @pl.when(unit != 2)
        def _():
            sum_copy(place, unit, TILE).wait_recv()
            subtract(mate_tile(place, unit), 0, TILE, sums_in[place, unit])

        @pl.when(unit == 2)
        def _():
            sum_copy(place, unit, plain).wait_recv()
            subtract(mate_tile(place, unit), 0, plain, sums_in[place, unit, 0:plain])

    def shared_tile(place):
        subtract(mate_tile(place, 2), plain, SHARED, product(factor(shared[place]), 0))

    def pair(i, compute):
        s, unit = i // 3 + 1, lax.rem(i, 3)

        def one(d, carry):
            compute(place_of(d, s), unit)
            return carry

        lax.fori_loop(0, 2, one, 0)

    def visit(i, carry):
        s, unit = i // 3 + 1, lax.rem(i, 3)

        @pl.when(s > 1)
        def _():
            for d in (0, 1):
                arrived(d, s, unit)

                @pl.when(s == 2)
                def _():
                    ring_copy(d, s, unit, False).start()

                @pl.when(s == 3)
                def _():
                    ring_copy(d, s, unit, True).start()

        pair(i, column_tile)

        @pl.when(s == 2)
        def _():
            local_tile(unit)

        @pl.when(i > 0)
        def _():
            pair(i - 1, finish)

        @pl.when(unit == 2)
        def _():
            for d in (0, 1):
                arrived(d, s, 3)

                @pl.when(s < 3)
                def _():
                    ring_copy(d, s, 3, False).start()

                @pl.when(s == 3)
                def _():
                    ring_copy(d, s, 3, True).start()

            def one(d, carry):
                shared_tile(place_of(d, s))
                return carry

            lax.fori_loop(0, 2, one, 0)

        return carry

    lax.fori_loop(0, 9, visit, 0)

    far = lax.rem(z + 4, 8)

    def last(unit, carry):
        for d in (0, 1):
            arrived(d, 4, unit, True)
        column_tile(far, unit)

        @pl.when(unit == 0)
        def _():
            pair(8, finish)

        @pl.when(unit > 0)
        def _():
            finish(far, unit - 1)

        return carry

    lax.fori_loop(0, 3, last, 0)
    for d in (0, 1):
        arrived(d, 4, 3, True)
    shared_tile(far)
    finish(far, 2)

    for unit in range(4):
        mate_copy(unit).wait_send()
        for d in (0, 1):
            for s in range(4):
                ring_copy(d, s, unit, s == 3).wait_send()

    def drain(i, carry):
        place = lax.rem(z + i, 8)
        for unit in range(3):
            sum_copy(place, unit, plain if unit == 2 else TILE).wait_send()
        return carry

    lax.fori_loop(1, 8, drain, 0)
    pltpu.make_async_copy(pieces.at[pl.ds(0, peers)], pieces.at[pl.ds(0, peers)], spread_send).wait()

    @pl.when(z == 0)
    def _():
        ref = pieces.at[pl.ds(0, 7)]
        pltpu.make_async_copy(ref, ref, piece_sem.at[4]).wait()

    @pl.when(is_source)
    def _():
        ref = own.at[0, 0, pl.ds(0, 240)]
        pltpu.make_async_copy(ref, ref, piece_sem.at[0]).wait()

    @pl.when(is_couple)
    def _():
        ref = pieces.at[pl.ds(0, peers), :, pl.ds(512, 128)]
        pltpu.make_async_copy(ref, ref, piece_sem.at[2]).wait()


def shards(panel_cols, inverses, trailing):
    bf16 = jnp.bfloat16
    return pl.pallas_call(
        kernel,
        out_shape=pltpu.VMEM(trailing.shape, bf16),
        in_specs=[
            pl.BlockSpec(memory_space=pl.ANY),
            pl.BlockSpec(memory_space=pltpu.VMEM),
            pl.BlockSpec(memory_space=pl.ANY),
        ],
        out_specs=pl.BlockSpec(memory_space=pltpu.VMEM),
        scratch_shapes=[
            pltpu.VMEM((8, 3, TILE, 2 * TILE), bf16),
            pltpu.VMEM((3, TILE, 2 * TILE), bf16),
            pltpu.VMEM((8, SHARED, 2 * TILE), bf16),
            pltpu.VMEM((8, 3, TILE, TILE), bf16),
            pltpu.VMEM((8, 3, TILE, TILE), bf16),
            pltpu.VMEM((8, 16, 640), bf16),
            pltpu.VMEM((16, 128), bf16),
            pltpu.VMEM((2 * PIECE, 16, 640), bf16),
            pltpu.VMEM((TILE, TILE), bf16),
            pltpu.VMEM((2, TILE, 2 * TILE), bf16),
            pltpu.SemaphoreType.DMA((2, 4, 4)),
            pltpu.SemaphoreType.DMA((2, 4, 4)),
            pltpu.SemaphoreType.DMA((4,)),
            pltpu.SemaphoreType.DMA((4,)),
            pltpu.SemaphoreType.DMA((8, 3)),
            pltpu.SemaphoreType.DMA((8, 3)),
            pltpu.SemaphoreType.DMA((2,)),
            pltpu.SemaphoreType.DMA((6,)),
            pltpu.SemaphoreType.DMA,
            pltpu.SemaphoreType.DMA,
        ],
        compiler_params=pltpu.CompilerParams(
            collective_id=0, has_side_effects=True, vmem_limit_bytes=56 << 20
        ),
        name="panel_update",
    )(panel_cols, inverses, trailing)


def solution(mesh):
    in_specs = (P("col", "row", None), P(), P(None, "row", "col"))
    out_specs = P(None, "row", "col")
    return jax.shard_map(shards, mesh=mesh, in_specs=in_specs, out_specs=out_specs, check_vma=False)
```

```python
import functools

import jax
import jax.numpy as jnp
from jax import lax
from jax.experimental import pallas as pl
from jax.experimental.pallas import tpu as pltpu
from jax.sharding import PartitionSpec as P

MESH = pl.DeviceIdType.MESH
TILE = 256
SHARED = 128
FIRST = (0,)
FORWARD_FIRST = True
PIECE = 16


def times_transposed(left, right):
    return lax.dot_general(left, right, (((1,), (1,)), ((), ())), preferred_element_type=jnp.float32)


def kernel(
    panel, inverses, trailing, window,
    own, mate, shared, sums_in, sums_out, stage, couple_piece, pieces, couple, keys,
    ring_send, ring_recv, mate_send, mate_recv, sum_send, sum_recv,
    load_sem, piece_sem, spread_sem, ready_sem,
):
    row, col = lax.axis_index("row"), lax.axis_index("col")
    z, y = col // 2, lax.rem(col, 2)
    chip, core = row // 2, lax.rem(row, 2)
    my_piece = core * PIECE + chip * 2 + y
    mate_dev = (row, col + 1 - 2 * y)
    core_dev = (row + 1 - 2 * core, col)
    ring_dev = ((row, lax.rem(col + 2, 16)), (row, lax.rem(col + 14, 16)))
    plain = TILE - SHARED

    load_own = pltpu.make_async_copy(panel, own.at[z], load_sem.at[0])
    load_window = pltpu.make_async_copy(trailing, window, load_sem.at[1])
    load_own.start()
    load_window.start()

    def plane_device(q, plane):
        at = lax.rem(q, PIECE)
        return ((at // 2) * 2 + q // PIECE, plane * 2 + lax.rem(at, 2))

    key_plane = lax.rem(row + 14, 16) // 2
    is_source = col == 0
    is_couple = jnp.logical_and(is_source, row == 1)

    barrier = pltpu.get_barrier_semaphore()

    def greet(dev):
        pl.semaphore_signal(barrier, inc=1, device_id=dev, device_id_type=MESH)

    def greet_plane(p, carry):
        @pl.when(core * PIECE + p != my_piece)
        def _():
            greet(plane_device(core * PIECE + p, z))

        return carry

    lax.fori_loop(0, PIECE, greet_plane, 0)
    greet(core_dev)

    @pl.when(jnp.logical_and(jnp.logical_and(z == 0, core == 0), row + col > 0))
    def _():
        greet((1, 0))

    @pl.when(z == 0)
    def _():
        def greet_place(place, carry):
            greet((row, place * 2 + y))
            return carry

        lax.fori_loop(1, 8, greet_place, 0)

    @pl.when(jnp.logical_and(z != 0, z != 7))
    def _():
        greet(ring_dev[0])

    @pl.when(z > 1)
    def _():
        greet(ring_dev[1])

    beside = jnp.logical_or(z == 1, z == 7)
    from_others = jnp.where(z == 0, 0, jnp.where(beside, 2, 3))
    pl.semaphore_wait(barrier, 16 + from_others + jnp.where(is_couple, 15, 0))

    @pl.when(z != 0)
    def _():
        pl.semaphore_signal(
            ready_sem.at[jnp.where(beside, 0, 1)], inc=1, device_id=(row, y), device_id_type=MESH
        )

    load_own.wait()

    def is_shared(unit):
        return isinstance(unit, int) and unit == 3

    def ring_ref(d, s, unit):
        place = lax.rem(z + 8 - s, 8) if d == 0 else lax.rem(z + s, 8)
        return shared.at[place] if is_shared(unit) else own.at[place, unit]

    def ring_copy(d, s, unit, half):
        ref = ring_ref(d, s, unit)
        if half:
            rows = (SHARED if is_shared(unit) else TILE) // 2
            ref = ref.at[pl.ds(d * rows, rows)]
        return pltpu.make_async_remote_copy(
            ref, ref, ring_send.at[d, s, unit], ring_recv.at[d, s, unit],
            device_id=ring_dev[d], device_id_type=MESH,
        )

    def arrived(d, s, unit, half=False):
        ref = ring_ref(d, s, unit)
        if half:
            rows = (SHARED if is_shared(unit) else TILE) // 2
            ref = ref.at[pl.ds(d * rows, rows)]
        pltpu.make_async_remote_copy(
            ref, ref, ring_send.at[d, s - 1, unit], ring_recv.at[d, s - 1, unit],
            device_id=ring_dev[d], device_id_type=MESH,
        ).wait_recv()

    def mate_copy(unit):
        if unit == 3:
            ref, dst = own.at[z, 2, pl.ds(plain, SHARED)], shared.at[z]
        elif unit == 2:
            ref, dst = own.at[z, 2, pl.ds(0, plain)], mate.at[2, pl.ds(0, plain)]
        else:
            ref, dst = own.at[z, unit], mate.at[unit]
        return pltpu.make_async_remote_copy(
            ref, dst, mate_send.at[unit], mate_recv.at[unit], device_id=mate_dev, device_id_type=MESH
        )

    key_tile = jnp.where(row < 2, 1, 0)

    @pl.when(is_couple)
    def _():
        def send(q, carry):
            src = own.at[0, 0, pl.ds(lax.rem(q, PIECE) * 16, 16), pl.ds((q // PIECE) * 128, 128)]

            @pl.when(q != my_piece)
            def _():
                pltpu.make_async_remote_copy(
                    src, couple_piece, piece_sem.at[2], piece_sem.at[3], device_id=plane_device(q, 0),
                    device_id_type=MESH,
                ).start()

            @pl.when(q == my_piece)
            def _():
                pltpu.make_async_copy(src, couple_piece, piece_sem.at[3]).start()

            return carry

        lax.fori_loop(0, 2 * PIECE, send, 0)

    @pl.when(is_source)
    def _():
        def send(p, carry):
            q = core * PIECE + p
            src = own.at[0, key_tile, pl.ds(p * 16, 16)]
            dst = stage.at[key_plane, :, pl.ds(0, 512)]

            @pl.when(q != my_piece)
            def _():
                pltpu.make_async_remote_copy(
                    src, dst, piece_sem.at[0], piece_sem.at[1], device_id=plane_device(q, 0), device_id_type=MESH
                ).start()

            @pl.when(q == my_piece)
            def _():
                pltpu.make_async_copy(src, dst, piece_sem.at[1]).start()

            return carry

        lax.fori_loop(0, PIECE, send, 0)

    def begin(units):
        for unit in units:
            for d in (0, 1):
                ring_copy(d, 0, unit, False).start()

    mine = pieces.at[my_piece]

    def spread():
        def send(p, carry):
            q = core * PIECE + p

            @pl.when(q != my_piece)
            def _():
                pltpu.make_async_remote_copy(
                    mine, mine, spread_sem.at[0], spread_sem.at[1], device_id=plane_device(q, z), device_id_type=MESH
                ).start()

            return carry

        lax.fori_loop(0, PIECE, send, 0)

    for unit in (3, 0, 1, 2):
        mate_copy(unit).start()

    @pl.when(z == 0)
    def _():
        pl.semaphore_wait(ready_sem.at[0], 2)
        begin(FIRST)
        staged = stage.at[:, :, pl.ds(0, 512)]
        pltpu.make_async_copy(couple_piece, couple_piece, piece_sem.at[3]).wait()
        pltpu.make_async_copy(staged, staged, piece_sem.at[1]).wait()
        for plane in range(8):
            stage[plane, :, 512:640] = couple_piece[...]
        pieces[my_piece] = stage[0]
        pl.semaphore_wait(ready_sem.at[1], 5)

        def send(plane, carry):
            pltpu.make_async_remote_copy(
                stage.at[plane], mine, piece_sem.at[4], piece_sem.at[5], device_id=(row, plane * 2 + y),
                device_id_type=MESH,
            ).start()
            return carry

        lax.fori_loop(1, 8, send, 0)
        spread()
        begin([unit for unit in (0, 1, 2) if unit not in FIRST])

    @pl.when(z != 0)
    def _():
        begin((0, 1, 2))

    mate_copy(3).wait_recv()
    begin((3,))

    @pl.when(z != 0)
    def _():
        pltpu.make_async_copy(mine, mine, piece_sem.at[5]).wait()
        spread()

    peers = pieces.at[pl.ds(0, PIECE - 1)]
    half = pieces.at[pl.ds(core * PIECE, PIECE)]
    swap = pltpu.make_async_remote_copy(
        half, half, spread_sem.at[2], spread_sem.at[3], device_id=core_dev, device_id_type=MESH
    )

    for d in (0, 1):
        arrived(d, 1, 0)
        ring_copy(d, 1, 0, False).start()
    pltpu.make_async_copy(peers, peers, spread_sem.at[1]).wait()
    swap.start()
    for unit in (1, 2):
        for d in (0, 1):
            if FORWARD_FIRST:
                arrived(d, 1, unit)
                ring_copy(d, 1, unit, False).start()
    swap.wait_recv()

    for part in (0, 1):
        raw = pieces[part * PIECE:(part + 1) * PIECE, :, 512:640].reshape(TILE, 128)
        keys[0, :, part * 128:(part + 1) * 128] = raw
    couple[...] = times_transposed(keys[0, :, 0:TILE], inverses[0]).astype(jnp.bfloat16)

    def factor(raw):
        left = times_transposed(raw[:, 0:TILE], inverses[0]).astype(jnp.bfloat16)
        reduced = (raw[:, TILE:].astype(jnp.float32) - times_transposed(left, couple[...])).astype(jnp.bfloat16)
        right = times_transposed(reduced, inverses[1]).astype(jnp.bfloat16)
        return left, right

    def product(factors, which):
        left, right = factors
        return times_transposed(left, keys[which, :, 0:TILE]) + times_transposed(right, keys[which, :, TILE:])

    for which in (0, 1):
        parity = y if which == 0 else 1 - y
        raw = pieces[pl.ds(parity * PIECE, PIECE), :, 0:512].reshape(TILE, 2 * TILE)
        left, right = factor(raw)
        keys[which, :, 0:TILE] = left
        keys[which, :, TILE:] = right

    load_window.wait()

    def subtract(tile, start, rows, amount):
        at = (tile, pl.ds(start, rows))
        window[at] = (window[at].astype(jnp.float32) - amount.astype(jnp.float32)).astype(jnp.bfloat16)

    def own_tile(place, unit):
        return (place * 2 + y) * 3 + unit

    def mate_tile(place, unit):
        return (place * 2 + 1 - y) * 3 + unit

    mate[2, plain:TILE] = shared[z]

    def local_tile(unit):
        subtract(own_tile(z, unit), 0, TILE, product(factor(own[z, unit]), 0))
        subtract(mate_tile(z, unit), 0, TILE, product(factor(mate[unit]), 0))

    def place_of(d, s):
        return lax.rem(z + jnp.where(d == 0, 8 - s, s), 8)

    def sum_copy(place, unit, rows):
        return pltpu.make_async_remote_copy(
            sums_out.at[place, unit, pl.ds(0, rows)], sums_in.at[place, unit, pl.ds(0, rows)],
            sum_send.at[place, unit], sum_recv.at[place, unit], device_id=mate_dev, device_id_type=MESH,
        )

    def column_tile(place, unit):
        factors = factor(own[place, unit])
        sums_out[place, unit] = product(factors, 1).astype(jnp.bfloat16)

        @pl.when(unit != 2)
        def _():
            sum_copy(place, unit, TILE).start()

        @pl.when(unit == 2)
        def _():
            sum_copy(place, unit, plain).start()

        subtract(own_tile(place, unit), 0, TILE, product(factors, 0))

    def finish(place, unit):
        @pl.when(unit != 2)
        def _():
            sum_copy(place, unit, TILE).wait_recv()
            subtract(mate_tile(place, unit), 0, TILE, sums_in[place, unit])

        @pl.when(unit == 2)
        def _():
            sum_copy(place, unit, plain).wait_recv()
            subtract(mate_tile(place, unit), 0, plain, sums_in[place, unit, 0:plain])

    def shared_tile(place):
        subtract(mate_tile(place, 2), plain, SHARED, product(factor(shared[place]), 0))

    def pair(i, compute):
        s, unit = i // 3 + 1, lax.rem(i, 3)

        def one(d, carry):
            compute(place_of(d, s), unit)
            return carry

        lax.fori_loop(0, 2, one, 0)

    def visit(i, carry):
        s, unit = i // 3 + 1, lax.rem(i, 3)

        @pl.when(i >= (3 if FORWARD_FIRST else 1))
        def _():
            for d in (0, 1):
                arrived(d, s, unit)

                @pl.when(s < 3)
                def _():
                    ring_copy(d, s, unit, False).start()

                @pl.when(s == 3)
                def _():
                    ring_copy(d, s, unit, True).start()

        pair(i, column_tile)

        @pl.when(i == 3)
        def _():
            for u in (0, 1, 2):
                mate_copy(u).wait_recv()

        @pl.when(s == 2)
        def _():
            local_tile(unit)

        @pl.when(i > 0)
        def _():
            pair(i - 1, finish)

        @pl.when(unit == 2)
        def _():
            for d in (0, 1):
                arrived(d, s, 3)

                @pl.when(s < 3)
                def _():
                    ring_copy(d, s, 3, False).start()

                @pl.when(s == 3)
                def _():
                    ring_copy(d, s, 3, True).start()

            def one(d, carry):
                shared_tile(place_of(d, s))
                return carry

            lax.fori_loop(0, 2, one, 0)

        return carry

    lax.fori_loop(0, 9, visit, 0)

    far = lax.rem(z + 4, 8)

    def last(unit, carry):
        for d in (0, 1):
            arrived(d, 4, unit, True)
        column_tile(far, unit)

        @pl.when(unit == 0)
        def _():
            pair(8, finish)

        @pl.when(unit > 0)
        def _():
            finish(far, unit - 1)

        return carry

    lax.fori_loop(0, 3, last, 0)
    for d in (0, 1):
        arrived(d, 4, 3, True)
    shared_tile(far)
    finish(far, 2)

    for unit in range(4):
        mate_copy(unit).wait_send()
        for d in (0, 1):
            for s in range(4):
                ring_copy(d, s, unit, s == 3).wait_send()

    def drain(i, carry):
        place = lax.rem(z + i, 8)
        for unit in range(3):
            sum_copy(place, unit, plain if unit == 2 else TILE).wait_send()
        return carry

    lax.fori_loop(1, 8, drain, 0)
    pltpu.make_async_copy(peers, peers, spread_sem.at[0]).wait()
    swap.wait_send()

    @pl.when(z == 0)
    def _():
        ref = pieces.at[pl.ds(0, 7)]
        pltpu.make_async_copy(ref, ref, piece_sem.at[4]).wait()

    @pl.when(is_source)
    def _():
        ref = own.at[0, 0, pl.ds(0, 240)]
        pltpu.make_async_copy(ref, ref, piece_sem.at[0]).wait()

    @pl.when(is_couple)
    def _():
        ref = pieces.at[pl.ds(0, 2 * PIECE - 1), :, pl.ds(512, 128)]
        pltpu.make_async_copy(ref, ref, piece_sem.at[2]).wait()


def shards(panel_cols, inverses, trailing):
    bf16 = jnp.bfloat16
    return pl.pallas_call(
        kernel,
        out_shape=pltpu.VMEM(trailing.shape, bf16),
        in_specs=[
            pl.BlockSpec(memory_space=pl.ANY),
            pl.BlockSpec(memory_space=pltpu.VMEM),
            pl.BlockSpec(memory_space=pl.ANY),
        ],
        out_specs=pl.BlockSpec(memory_space=pltpu.VMEM),
        scratch_shapes=[
            pltpu.VMEM((8, 3, TILE, 2 * TILE), bf16),
            pltpu.VMEM((3, TILE, 2 * TILE), bf16),
            pltpu.VMEM((8, SHARED, 2 * TILE), bf16),
            pltpu.VMEM((8, 3, TILE, TILE), bf16),
            pltpu.VMEM((8, 3, TILE, TILE), bf16),
            pltpu.VMEM((8, 16, 640), bf16),
            pltpu.VMEM((16, 128), bf16),
            pltpu.VMEM((2 * PIECE, 16, 640), bf16),
            pltpu.VMEM((TILE, TILE), bf16),
            pltpu.VMEM((2, TILE, 2 * TILE), bf16),
            pltpu.SemaphoreType.DMA((2, 4, 4)),
            pltpu.SemaphoreType.DMA((2, 4, 4)),
            pltpu.SemaphoreType.DMA((4,)),
            pltpu.SemaphoreType.DMA((4,)),
            pltpu.SemaphoreType.DMA((8, 3)),
            pltpu.SemaphoreType.DMA((8, 3)),
            pltpu.SemaphoreType.DMA((2,)),
            pltpu.SemaphoreType.DMA((6,)),
            pltpu.SemaphoreType.DMA((4,)),
            pltpu.SemaphoreType.REGULAR((2,)),
        ],
        compiler_params=pltpu.CompilerParams(
            collective_id=0, has_side_effects=True, vmem_limit_bytes=56 << 20
        ),
        name="panel_update",
    )(panel_cols, inverses, trailing)


def solution(mesh):
    in_specs = (P("col", "row", None), P(), P(None, "row", "col"))
    out_specs = P(None, "row", "col")
    return jax.shard_map(shards, mesh=mesh, in_specs=in_specs, out_specs=out_specs, check_vma=False)
```

```python
import functools

import jax
import jax.numpy as jnp
from jax import lax
from jax.experimental import pallas as pl
from jax.experimental.pallas import tpu as pltpu
from jax.sharding import PartitionSpec as P

MESH = pl.DeviceIdType.MESH
TILE = 256
SHARED = 128
FIRST = 128
FEWER = 64
BEFORE = (3, 0)
PIECE = 16


def times_transposed(left, right):
    return lax.dot_general(left, right, (((1,), (1,)), ((), ())), preferred_element_type=jnp.float32)


def kernel(
    panel, inverses, trailing, window,
    own, mate, shared, sums_in, sums_out, stage, couple_piece, pieces, couple, keys,
    ring_send, ring_recv, mate_send, mate_recv, sum_send, sum_recv,
    load_sem, piece_sem, spread_sem, ready_sem,
):
    row, col = lax.axis_index("row"), lax.axis_index("col")
    z, y = col // 2, lax.rem(col, 2)
    chip, core = row // 2, lax.rem(row, 2)
    my_piece = core * PIECE + chip * 2 + y
    mate_dev = (row, col + 1 - 2 * y)
    core_dev = (row + 1 - 2 * core, col)
    ring_dev = ((row, lax.rem(col + 2, 16)), (row, lax.rem(col + 14, 16)))
    plain = TILE - SHARED

    load_own = pltpu.make_async_copy(panel, own.at[z], load_sem.at[0])
    load_window = pltpu.make_async_copy(trailing, window, load_sem.at[1])
    load_own.start()
    load_window.start()

    def plane_device(q, plane):
        at = lax.rem(q, PIECE)
        return ((at // 2) * 2 + q // PIECE, plane * 2 + lax.rem(at, 2))

    key_plane = lax.rem(row + 14, 16) // 2
    is_source = col == 0
    is_couple = jnp.logical_and(is_source, row == 1)

    barrier = pltpu.get_barrier_semaphore()

    def greet(dev):
        pl.semaphore_signal(barrier, inc=1, device_id=dev, device_id_type=MESH)

    def greet_plane(p, carry):
        @pl.when(core * PIECE + p != my_piece)
        def _():
            greet(plane_device(core * PIECE + p, z))

        return carry

    lax.fori_loop(0, PIECE, greet_plane, 0)
    greet(core_dev)

    @pl.when(jnp.logical_and(jnp.logical_and(z == 0, core == 0), row + col > 0))
    def _():
        greet((1, 0))

    @pl.when(z == 0)
    def _():
        def greet_place(place, carry):
            greet((row, place * 2 + y))
            return carry

        lax.fori_loop(1, 8, greet_place, 0)

    @pl.when(jnp.logical_and(z != 0, z != 7))
    def _():
        greet(ring_dev[0])

    @pl.when(z > 1)
    def _():
        greet(ring_dev[1])

    beside = jnp.logical_or(z == 1, z == 7)
    from_others = jnp.where(z == 0, 0, jnp.where(beside, 2, 3))
    pl.semaphore_wait(barrier, 16 + from_others + jnp.where(is_couple, 15, 0))

    @pl.when(z != 0)
    def _():
        pl.semaphore_signal(
            ready_sem.at[jnp.where(beside, 0, 1)], inc=1, device_id=(row, y), device_id_type=MESH
        )

    load_own.wait()

    def is_shared(unit):
        return isinstance(unit, int) and unit == 3

    def ring_ref(d, s, unit):
        place = lax.rem(z + 8 - s, 8) if d == 0 else lax.rem(z + s, 8)
        return shared.at[place] if is_shared(unit) else own.at[place, unit]

    def ring_copy(d, s, unit, up=None):
        ref = ring_ref(d, s, unit)
        if up is not None:
            rows = SHARED if is_shared(unit) else TILE
            up = up * rows // TILE
            ref = ref.at[pl.ds(0, up)] if d == 0 else ref.at[pl.ds(up, rows - up)]
        return pltpu.make_async_remote_copy(
            ref, ref, ring_send.at[d, s, unit], ring_recv.at[d, s, unit],
            device_id=ring_dev[d], device_id_type=MESH,
        )

    def arrived(d, s, unit, up=None):
        ref = ring_ref(d, s, unit)
        if up is not None:
            rows = SHARED if is_shared(unit) else TILE
            up = up * rows // TILE
            ref = ref.at[pl.ds(0, up)] if d == 0 else ref.at[pl.ds(up, rows - up)]
        pltpu.make_async_remote_copy(
            ref, ref, ring_send.at[d, s - 1, unit], ring_recv.at[d, s - 1, unit],
            device_id=ring_dev[d], device_id_type=MESH,
        ).wait_recv()

    def opposite(place, action):
        @pl.when(place == 1)
        def _():
            action(FEWER)

        @pl.when(place == 7)
        def _():
            action(TILE - FEWER)

        @pl.when(jnp.logical_and(place != 1, place != 7))
        def _():
            action(TILE // 2)

    next_place = (lax.rem(z + 1, 8), lax.rem(z + 7, 8))

    def mate_copy(unit):
        if unit == 3:
            ref, dst = own.at[z, 2, pl.ds(plain, SHARED)], shared.at[z]
        else:
            ref, dst = own.at[z, unit], mate.at[unit]
        return pltpu.make_async_remote_copy(
            ref, dst, mate_send.at[unit], mate_recv.at[unit], device_id=mate_dev, device_id_type=MESH
        )

    key_tile = jnp.where(row < 2, 1, 0)

    @pl.when(is_couple)
    def _():
        def send(q, carry):
            src = own.at[0, 0, pl.ds(lax.rem(q, PIECE) * 16, 16), pl.ds((q // PIECE) * 128, 128)]

            @pl.when(q != my_piece)
            def _():
                pltpu.make_async_remote_copy(
                    src, couple_piece, piece_sem.at[2], piece_sem.at[3], device_id=plane_device(q, 0),
                    device_id_type=MESH,
                ).start()

            @pl.when(q == my_piece)
            def _():
                pltpu.make_async_copy(src, couple_piece, piece_sem.at[3]).start()

            return carry

        lax.fori_loop(0, 2 * PIECE, send, 0)

    @pl.when(is_source)
    def _():
        def send(p, carry):
            q = core * PIECE + p
            src = own.at[0, key_tile, pl.ds(p * 16, 16)]
            dst = stage.at[key_plane, :, pl.ds(0, 512)]

            @pl.when(q != my_piece)
            def _():
                pltpu.make_async_remote_copy(
                    src, dst, piece_sem.at[0], piece_sem.at[1], device_id=plane_device(q, 0), device_id_type=MESH
                ).start()

            @pl.when(q == my_piece)
            def _():
                pltpu.make_async_copy(src, dst, piece_sem.at[1]).start()

            return carry

        lax.fori_loop(0, PIECE, send, 0)

    def begin(units):
        for unit in units:
            for d in (0, 1):
                ring_copy(d, 0, unit).start()

    def begin_part(start, rows):
        if rows:
            for d in (0, 1):
                ref = own.at[z, 0, pl.ds(start, rows)]
                pltpu.make_async_remote_copy(
                    ref, ref, ring_send.at[d, 0, 0], ring_recv.at[d, 0, 0], device_id=ring_dev[d], device_id_type=MESH
                ).start()

    mine = pieces.at[my_piece]

    def spread():
        def send(p, carry):
            q = core * PIECE + p

            @pl.when(q != my_piece)
            def _():
                pltpu.make_async_remote_copy(
                    mine, mine, spread_sem.at[0], spread_sem.at[1], device_id=plane_device(q, z), device_id_type=MESH
                ).start()

            return carry

        lax.fori_loop(0, PIECE, send, 0)
        for unit in (0, 1):
            if unit not in BEFORE:
                mate_copy(unit).start()

    for unit in BEFORE:
        mate_copy(unit).start()

    @pl.when(z == 0)
    def _():
        pl.semaphore_wait(ready_sem.at[0], 2)
        begin_part(0, FIRST)
        staged = stage.at[:, :, pl.ds(0, 512)]
        pltpu.make_async_copy(couple_piece, couple_piece, piece_sem.at[3]).wait()
        pltpu.make_async_copy(staged, staged, piece_sem.at[1]).wait()
        for plane in range(8):
            stage[plane, :, 512:640] = couple_piece[...]
        pieces[my_piece] = stage[0]
        pl.semaphore_wait(ready_sem.at[1], 5)

        def send(plane, carry):
            pltpu.make_async_remote_copy(
                stage.at[plane], mine, piece_sem.at[4], piece_sem.at[5], device_id=(row, plane * 2 + y),
                device_id_type=MESH,
            ).start()
            return carry

        lax.fori_loop(1, 8, send, 0)
        begin_part(FIRST, TILE - FIRST)
        begin((1, 2))
        spread()

    @pl.when(z != 0)
    def _():
        begin((0, 1, 2))

    mate_copy(3).wait_recv()
    begin((3,))

    @pl.when(z != 0)
    def _():
        pltpu.make_async_copy(mine, mine, piece_sem.at[5]).wait()
        spread()

    peers = pieces.at[pl.ds(0, PIECE - 1)]
    half = pieces.at[pl.ds(core * PIECE, PIECE)]
    swap = pltpu.make_async_remote_copy(
        half, half, spread_sem.at[2], spread_sem.at[3], device_id=core_dev, device_id_type=MESH
    )

    for d in (0, 1):
        arrived(d, 1, 0)
        ring_copy(d, 1, 0).start()
    pltpu.make_async_copy(peers, peers, spread_sem.at[1]).wait()
    swap.start()
    for unit in (1, 2):
        for d in (0, 1):
            arrived(d, 1, unit)
            ring_copy(d, 1, unit).start()
    swap.wait_recv()

    for part in (0, 1):
        raw = pieces[part * PIECE:(part + 1) * PIECE, :, 512:640].reshape(TILE, 128)
        keys[0, :, part * 128:(part + 1) * 128] = raw
    couple[...] = times_transposed(keys[0, :, 0:TILE], inverses[0]).astype(jnp.bfloat16)

    def factor(raw):
        left = times_transposed(raw[:, 0:TILE], inverses[0]).astype(jnp.bfloat16)
        reduced = (raw[:, TILE:].astype(jnp.float32) - times_transposed(left, couple[...])).astype(jnp.bfloat16)
        right = times_transposed(reduced, inverses[1]).astype(jnp.bfloat16)
        return left, right

    def product(factors, which):
        left, right = factors
        return times_transposed(left, keys[which, :, 0:TILE]) + times_transposed(right, keys[which, :, TILE:])

    for which in (0, 1):
        parity = y if which == 0 else 1 - y
        raw = pieces[pl.ds(parity * PIECE, PIECE), :, 0:512].reshape(TILE, 2 * TILE)
        left, right = factor(raw)
        keys[which, :, 0:TILE] = left
        keys[which, :, TILE:] = right

    load_window.wait()

    def subtract(tile, start, rows, amount):
        at = (tile, pl.ds(start, rows))
        window[at] = (window[at].astype(jnp.float32) - amount.astype(jnp.float32)).astype(jnp.bfloat16)

    def own_tile(place, unit):
        return (place * 2 + y) * 3 + unit

    def mate_tile(place, unit):
        return (place * 2 + 1 - y) * 3 + unit

    def local_tile(unit):
        subtract(own_tile(z, unit), 0, TILE, product(factor(own[z, unit]), 0))
        subtract(mate_tile(z, unit), 0, TILE, product(factor(mate[unit]), 0))

    def place_of(d, s):
        return lax.rem(z + jnp.where(d == 0, 8 - s, s), 8)

    def sum_copy(place, unit, rows):
        return pltpu.make_async_remote_copy(
            sums_out.at[place, unit, pl.ds(0, rows)], sums_in.at[place, unit, pl.ds(0, rows)],
            sum_send.at[place, unit], sum_recv.at[place, unit], device_id=mate_dev, device_id_type=MESH,
        )

    def column_tile(place, unit):
        factors = factor(own[place, unit])
        sums_out[place, unit] = product(factors, 1).astype(jnp.bfloat16)

        @pl.when(unit != 2)
        def _():
            sum_copy(place, unit, TILE).start()

        @pl.when(unit == 2)
        def _():
            sum_copy(place, unit, plain).start()

        subtract(own_tile(place, unit), 0, TILE, product(factors, 0))

    def finish(place, unit):
        @pl.when(unit != 2)
        def _():
            sum_copy(place, unit, TILE).wait_recv()
            subtract(mate_tile(place, unit), 0, TILE, sums_in[place, unit])

        @pl.when(unit == 2)
        def _():
            sum_copy(place, unit, plain).wait_recv()
            subtract(mate_tile(place, unit), 0, plain, sums_in[place, unit, 0:plain])

    def shared_tile(place):
        subtract(mate_tile(place, 2), plain, SHARED, product(factor(shared[place]), 0))

    def pair(i, compute):
        s, unit = i // 3 + 1, lax.rem(i, 3)

        def one(d, carry):
            compute(place_of(d, s), unit)
            return carry

        lax.fori_loop(0, 2, one, 0)

    def visit(i, carry):
        s, unit = i // 3 + 1, lax.rem(i, 3)

        @pl.when(s > 1)
        def _():
            for d in (0, 1):
                arrived(d, s, unit)

                @pl.when(s == 2)
                def _():
                    ring_copy(d, s, unit).start()

                @pl.when(s == 3)
                def _():
                    opposite(next_place[d], lambda up: ring_copy(d, s, unit, up).start())

        pair(i, column_tile)

        @pl.when(i == 3)
        def _():
            mate_copy(0).wait_recv()
            mate_copy(1).wait_recv()

        @pl.when(jnp.logical_and(s == 2, unit != 2))
        def _():
            local_tile(unit)

        @pl.when(i == 5)
        def _():
            finish(z, 2)
            shared_tile(z)

        @pl.when(i > 0)
        def _():
            pair(i - 1, finish)

        @pl.when(unit == 2)
        def _():
            for d in (0, 1):
                arrived(d, s, 3)

                @pl.when(s < 3)
                def _():
                    ring_copy(d, s, 3).start()

                @pl.when(s == 3)
                def _():
                    opposite(next_place[d], lambda up: ring_copy(d, s, 3, up).start())

            def one(d, carry):
                shared_tile(place_of(d, s))
                return carry

            lax.fori_loop(0, 2, one, 0)

        return carry

    column_tile(z, 2)
    lax.fori_loop(0, 9, visit, 0)

    far = lax.rem(z + 4, 8)

    def last(unit, carry):
        for d in (0, 1):
            opposite(z, lambda up: arrived(d, 4, unit, up))
        column_tile(far, unit)

        @pl.when(unit == 0)
        def _():
            pair(8, finish)

        @pl.when(unit > 0)
        def _():
            finish(far, unit - 1)

        return carry

    lax.fori_loop(0, 3, last, 0)
    for d in (0, 1):
        opposite(z, lambda up: arrived(d, 4, 3, up))
    shared_tile(far)
    finish(far, 2)

    for unit in range(4):
        if unit != 2:
            mate_copy(unit).wait_send()
        for d in (0, 1):
            for s in range(3):
                ring_copy(d, s, unit).wait_send()
            opposite(next_place[d], lambda up: ring_copy(d, 3, unit, up).wait_send())

    def drain(i, carry):
        place = lax.rem(z + i, 8)
        for unit in range(3):
            sum_copy(place, unit, plain if unit == 2 else TILE).wait_send()
        return carry

    lax.fori_loop(1, 8, drain, 0)
    sum_copy(z, 2, plain).wait_send()
    pltpu.make_async_copy(peers, peers, spread_sem.at[0]).wait()
    swap.wait_send()

    @pl.when(z == 0)
    def _():
        ref = pieces.at[pl.ds(0, 7)]
        pltpu.make_async_copy(ref, ref, piece_sem.at[4]).wait()

    @pl.when(is_source)
    def _():
        ref = own.at[0, 0, pl.ds(0, 240)]
        pltpu.make_async_copy(ref, ref, piece_sem.at[0]).wait()

    @pl.when(is_couple)
    def _():
        ref = pieces.at[pl.ds(0, 2 * PIECE - 1), :, pl.ds(512, 128)]
        pltpu.make_async_copy(ref, ref, piece_sem.at[2]).wait()


def shards(panel_cols, inverses, trailing):
    bf16 = jnp.bfloat16
    return pl.pallas_call(
        kernel,
        out_shape=pltpu.VMEM(trailing.shape, bf16),
        in_specs=[
            pl.BlockSpec(memory_space=pl.ANY),
            pl.BlockSpec(memory_space=pltpu.VMEM),
            pl.BlockSpec(memory_space=pl.ANY),
        ],
        out_specs=pl.BlockSpec(memory_space=pltpu.VMEM),
        scratch_shapes=[
            pltpu.VMEM((8, 3, TILE, 2 * TILE), bf16),
            pltpu.VMEM((2, TILE, 2 * TILE), bf16),
            pltpu.VMEM((8, SHARED, 2 * TILE), bf16),
            pltpu.VMEM((8, 3, TILE, TILE), bf16),
            pltpu.VMEM((8, 3, TILE, TILE), bf16),
            pltpu.VMEM((8, 16, 640), bf16),
            pltpu.VMEM((16, 128), bf16),
            pltpu.VMEM((2 * PIECE, 16, 640), bf16),
            pltpu.VMEM((TILE, TILE), bf16),
            pltpu.VMEM((2, TILE, 2 * TILE), bf16),
            pltpu.SemaphoreType.DMA((2, 4, 4)),
            pltpu.SemaphoreType.DMA((2, 4, 4)),
            pltpu.SemaphoreType.DMA((4,)),
            pltpu.SemaphoreType.DMA((4,)),
            pltpu.SemaphoreType.DMA((8, 3)),
            pltpu.SemaphoreType.DMA((8, 3)),
            pltpu.SemaphoreType.DMA((2,)),
            pltpu.SemaphoreType.DMA((6,)),
            pltpu.SemaphoreType.DMA((4,)),
            pltpu.SemaphoreType.REGULAR((2,)),
        ],
        compiler_params=pltpu.CompilerParams(
            collective_id=0, has_side_effects=True, vmem_limit_bytes=56 << 20
        ),
        name="panel_update",
    )(panel_cols, inverses, trailing)


def solution(mesh):
    in_specs = (P("col", "row", None), P(), P(None, "row", "col"))
    out_specs = P(None, "row", "col")
    return jax.shard_map(shards, mesh=mesh, in_specs=in_specs, out_specs=out_specs, check_vma=False)
```

```python
import functools

import jax
import jax.numpy as jnp
from jax import lax
from jax.experimental import pallas as pl
from jax.experimental.pallas import tpu as pltpu
from jax.sharding import PartitionSpec as P

MESH = pl.DeviceIdType.MESH
TILE = 256
SHARED = 112
FIRST = 128
FEWER = 112
BEFORE = (3, 0)
PIECE = 16


def times_transposed(left, right):
    return lax.dot_general(left, right, (((1,), (1,)), ((), ())), preferred_element_type=jnp.float32)


def kernel(
    panel, inverses, trailing, window,
    own, mate, shared, sums_in, sums_out, stage, couple_piece, pieces, couple, keys,
    ring_send, ring_recv, mate_send, mate_recv, sum_send, sum_recv,
    load_sem, piece_sem, spread_sem, ready_sem,
):
    row, col = lax.axis_index("row"), lax.axis_index("col")
    z, y = col // 2, lax.rem(col, 2)
    chip, core = row // 2, lax.rem(row, 2)
    my_piece = core * PIECE + chip * 2 + y
    mate_dev = (row, col + 1 - 2 * y)
    core_dev = (row + 1 - 2 * core, col)
    ring_dev = ((row, lax.rem(col + 2, 16)), (row, lax.rem(col + 14, 16)))
    plain = TILE - SHARED

    load_own = pltpu.make_async_copy(panel, own.at[z], load_sem.at[0])
    load_window = pltpu.make_async_copy(trailing, window, load_sem.at[1])
    load_own.start()
    load_window.start()

    def plane_device(q, plane):
        at = lax.rem(q, PIECE)
        return ((at // 2) * 2 + q // PIECE, plane * 2 + lax.rem(at, 2))

    key_plane = lax.rem(row + 14, 16) // 2
    is_source = col == 0
    is_couple = jnp.logical_and(is_source, row == 1)

    barrier = pltpu.get_barrier_semaphore()

    def greet(dev):
        pl.semaphore_signal(barrier, inc=1, device_id=dev, device_id_type=MESH)

    @pl.when(z == 0)
    def _():
        def greet_place(place, carry):
            greet((row, place * 2 + y))
            return carry

        lax.fori_loop(1, 8, greet_place, 0)

    @pl.when(jnp.logical_and(z > 0, z < 6))
    def _():
        greet(ring_dev[0])

    @pl.when(z > 2)
    def _():
        greet(ring_dev[1])

    def greet_plane(p, carry):
        @pl.when(core * PIECE + p != my_piece)
        def _():
            greet(plane_device(core * PIECE + p, z))

        return carry

    lax.fori_loop(0, PIECE, greet_plane, 0)
    greet(core_dev)

    @pl.when(jnp.logical_and(jnp.logical_and(z == 0, core == 0), row + col > 0))
    def _():
        greet((1, 0))

    beside = jnp.logical_or(z == 1, z == 7)
    from_others = jnp.where(z == 0, 0, jnp.where(beside, 1, 3))
    pl.semaphore_wait(barrier, 16 + from_others + jnp.where(is_couple, 15, 0))

    @pl.when(z != 0)
    def _():
        pl.semaphore_signal(
            ready_sem.at[jnp.where(z == 1, 0, jnp.where(z == 7, 2, 1))], inc=1, device_id=(row, y), device_id_type=MESH
        )

    @pl.when(z == 2)
    def _():
        pl.semaphore_signal(ready_sem.at[3], inc=1, device_id=ring_dev[1], device_id_type=MESH)

    @pl.when(z == 6)
    def _():
        pl.semaphore_signal(ready_sem.at[3], inc=1, device_id=ring_dev[0], device_id_type=MESH)

    load_own.wait()

    def is_shared(unit):
        return isinstance(unit, int) and unit == 3

    def ring_ref(d, s, unit):
        place = lax.rem(z + 8 - s, 8) if d == 0 else lax.rem(z + s, 8)
        return shared.at[place] if is_shared(unit) else own.at[place, unit]

    def ring_copy(d, s, unit, up=None):
        ref = ring_ref(d, s, unit)
        if up is not None:
            rows = SHARED if is_shared(unit) else TILE
            up = up * rows // TILE // 16 * 16
            ref = ref.at[pl.ds(0, up)] if d == 0 else ref.at[pl.ds(up, rows - up)]
        return pltpu.make_async_remote_copy(
            ref, ref, ring_send.at[d, s, unit], ring_recv.at[d, s, unit],
            device_id=ring_dev[d], device_id_type=MESH,
        )

    def arrived(d, s, unit, up=None):
        ref = ring_ref(d, s, unit)
        if up is not None:
            rows = SHARED if is_shared(unit) else TILE
            up = up * rows // TILE // 16 * 16
            ref = ref.at[pl.ds(0, up)] if d == 0 else ref.at[pl.ds(up, rows - up)]
        pltpu.make_async_remote_copy(
            ref, ref, ring_send.at[d, s - 1, unit], ring_recv.at[d, s - 1, unit],
            device_id=ring_dev[d], device_id_type=MESH,
        ).wait_recv()

    def opposite(place, action):
        @pl.when(place == 1)
        def _():
            action(FEWER)

        @pl.when(place == 7)
        def _():
            action(TILE - FEWER)

        @pl.when(jnp.logical_and(place != 1, place != 7))
        def _():
            action(TILE // 2)

    next_place = (lax.rem(z + 1, 8), lax.rem(z + 7, 8))

    def mate_copy(unit):
        if unit == 3:
            ref, dst = own.at[z, 2, pl.ds(plain, SHARED)], shared.at[z]
        else:
            ref, dst = own.at[z, unit], mate.at[unit]
        return pltpu.make_async_remote_copy(
            ref, dst, mate_send.at[unit], mate_recv.at[unit], device_id=mate_dev, device_id_type=MESH
        )

    key_tile = jnp.where(row < 2, 1, 0)

    @pl.when(is_couple)
    def _():
        def send(q, carry):
            src = own.at[0, 0, pl.ds(lax.rem(q, PIECE) * 16, 16), pl.ds((q // PIECE) * 128, 128)]

            @pl.when(q != my_piece)
            def _():
                pltpu.make_async_remote_copy(
                    src, couple_piece, piece_sem.at[2], piece_sem.at[3], device_id=plane_device(q, 0),
                    device_id_type=MESH,
                ).start()

            @pl.when(q == my_piece)
            def _():
                pltpu.make_async_copy(src, couple_piece, piece_sem.at[3]).start()

            return carry

        lax.fori_loop(0, 2 * PIECE, send, 0)

    @pl.when(is_source)
    def _():
        def send(p, carry):
            q = core * PIECE + p
            src = own.at[0, key_tile, pl.ds(p * 16, 16)]
            dst = stage.at[key_plane, :, pl.ds(0, 512)]

            @pl.when(q != my_piece)
            def _():
                pltpu.make_async_remote_copy(
                    src, dst, piece_sem.at[0], piece_sem.at[1], device_id=plane_device(q, 0), device_id_type=MESH
                ).start()

            @pl.when(q == my_piece)
            def _():
                pltpu.make_async_copy(src, dst, piece_sem.at[1]).start()

            return carry

        lax.fori_loop(0, PIECE, send, 0)

    def begin(units, ways=(0, 1)):
        for unit in units:
            for d in ways:
                ring_copy(d, 0, unit).start()

    def begin_part(start, rows, ways=(0, 1)):
        if rows:
            for d in ways:
                ref = own.at[z, 0, pl.ds(start, rows)]
                pltpu.make_async_remote_copy(
                    ref, ref, ring_send.at[d, 0, 0], ring_recv.at[d, 0, 0], device_id=ring_dev[d], device_id_type=MESH
                ).start()

    mine = pieces.at[my_piece]

    def spread():
        def send(p, carry):
            q = core * PIECE + p

            @pl.when(q != my_piece)
            def _():
                pltpu.make_async_remote_copy(
                    mine, mine, spread_sem.at[0], spread_sem.at[1], device_id=plane_device(q, z), device_id_type=MESH
                ).start()

            return carry

        lax.fori_loop(0, PIECE, send, 0)
        for unit in (0, 1):
            if unit not in BEFORE:
                mate_copy(unit).start()

    def begin_mate():
        for unit in BEFORE:
            mate_copy(unit).start()

    @pl.when(z == 0)
    def _():
        begin_mate()
        pl.semaphore_wait(ready_sem.at[0], 1)
        begin_part(0, FIRST, (0,))
        pl.semaphore_wait(ready_sem.at[2], 1)
        begin_part(0, FIRST, (1,))
        staged = stage.at[:, :, pl.ds(0, 512)]
        pltpu.make_async_copy(couple_piece, couple_piece, piece_sem.at[3]).wait()
        pltpu.make_async_copy(staged, staged, piece_sem.at[1]).wait()
        for plane in range(8):
            stage[plane, :, 512:640] = couple_piece[...]
        pieces[my_piece] = stage[0]
        pl.semaphore_wait(ready_sem.at[1], 5)

        def send(plane, carry):
            pltpu.make_async_remote_copy(
                stage.at[plane], mine, piece_sem.at[4], piece_sem.at[5], device_id=(row, plane * 2 + y),
                device_id_type=MESH,
            ).start()
            return carry

        lax.fori_loop(1, 8, send, 0)
        begin_part(FIRST, TILE - FIRST)
        begin((1, 2))
        spread()

    def begin_beside(inward, outward):
        begin((0,), (inward,))
        begin_mate()
        begin((1, 2), (inward,))
        pl.semaphore_wait(ready_sem.at[3], 1)
        begin((0, 1, 2), (outward,))

    @pl.when(z == 1)
    def _():
        begin_beside(1, 0)

    @pl.when(z == 7)
    def _():
        begin_beside(0, 1)

    @pl.when(jnp.logical_and(z > 1, z < 7))
    def _():
        begin((0,))
        begin_mate()
        begin((1, 2))

    mate_copy(3).wait_recv()
    begin((3,))

    @pl.when(z != 0)
    def _():
        pltpu.make_async_copy(mine, mine, piece_sem.at[5]).wait()
        spread()

    peers = pieces.at[pl.ds(0, PIECE - 1)]
    half = pieces.at[pl.ds(core * PIECE, PIECE)]
    swap = pltpu.make_async_remote_copy(
        half, half, spread_sem.at[2], spread_sem.at[3], device_id=core_dev, device_id_type=MESH
    )

    for d in (0, 1):
        arrived(d, 1, 0)
        ring_copy(d, 1, 0).start()
    pltpu.make_async_copy(peers, peers, spread_sem.at[1]).wait()
    swap.start()
    for unit in (1, 2):
        for d in (0, 1):
            arrived(d, 1, unit)
            ring_copy(d, 1, unit).start()
    swap.wait_recv()

    for part in (0, 1):
        raw = pieces[part * PIECE:(part + 1) * PIECE, :, 512:640].reshape(TILE, 128)
        keys[0, :, part * 128:(part + 1) * 128] = raw
    couple[...] = times_transposed(keys[0, :, 0:TILE], inverses[0]).astype(jnp.bfloat16)

    def factor(raw):
        left = times_transposed(raw[:, 0:TILE], inverses[0]).astype(jnp.bfloat16)
        reduced = (raw[:, TILE:].astype(jnp.float32) - times_transposed(left, couple[...])).astype(jnp.bfloat16)
        right = times_transposed(reduced, inverses[1]).astype(jnp.bfloat16)
        return left, right

    def product(factors, which):
        left, right = factors
        return times_transposed(left, keys[which, :, 0:TILE]) + times_transposed(right, keys[which, :, TILE:])

    for which in (0, 1):
        parity = y if which == 0 else 1 - y
        raw = pieces[pl.ds(parity * PIECE, PIECE), :, 0:512].reshape(TILE, 2 * TILE)
        left, right = factor(raw)
        keys[which, :, 0:TILE] = left
        keys[which, :, TILE:] = right

    load_window.wait()

    def subtract(tile, start, rows, amount):
        at = (tile, pl.ds(start, rows))
        window[at] = (window[at].astype(jnp.float32) - amount.astype(jnp.float32)).astype(jnp.bfloat16)

    def own_tile(place, unit):
        return (place * 2 + y) * 3 + unit

    def mate_tile(place, unit):
        return (place * 2 + 1 - y) * 3 + unit

    def local_tile(unit):
        subtract(own_tile(z, unit), 0, TILE, product(factor(own[z, unit]), 0))
        subtract(mate_tile(z, unit), 0, TILE, product(factor(mate[unit]), 0))

    def place_of(d, s):
        return lax.rem(z + jnp.where(d == 0, 8 - s, s), 8)

    def sum_copy(place, unit, rows):
        return pltpu.make_async_remote_copy(
            sums_out.at[place, unit, pl.ds(0, rows)], sums_in.at[place, unit, pl.ds(0, rows)],
            sum_send.at[place, unit], sum_recv.at[place, unit], device_id=mate_dev, device_id_type=MESH,
        )

    def column_tile(place, unit):
        factors = factor(own[place, unit])
        sums_out[place, unit] = product(factors, 1).astype(jnp.bfloat16)

        @pl.when(unit != 2)
        def _():
            sum_copy(place, unit, TILE).start()

        @pl.when(unit == 2)
        def _():
            sum_copy(place, unit, plain).start()

        subtract(own_tile(place, unit), 0, TILE, product(factors, 0))

    def finish(place, unit):
        @pl.when(unit != 2)
        def _():
            sum_copy(place, unit, TILE).wait_recv()
            subtract(mate_tile(place, unit), 0, TILE, sums_in[place, unit])

        @pl.when(unit == 2)
        def _():
            sum_copy(place, unit, plain).wait_recv()
            subtract(mate_tile(place, unit), 0, plain, sums_in[place, unit, 0:plain])

    def shared_tile(place):
        subtract(mate_tile(place, 2), plain, SHARED, product(factor(shared[place]), 0))

    def pair(i, compute):
        s, unit = i // 3 + 1, lax.rem(i, 3)

        def one(d, carry):
            compute(place_of(d, s), unit)
            return carry

        lax.fori_loop(0, 2, one, 0)

    def visit(i, carry):
        s, unit = i // 3 + 1, lax.rem(i, 3)

        @pl.when(s > 1)
        def _():
            for d in (0, 1):
                arrived(d, s, unit)

                @pl.when(s == 2)
                def _():
                    ring_copy(d, s, unit).start()

                @pl.when(s == 3)
                def _():
                    opposite(next_place[d], lambda up: ring_copy(d, s, unit, up).start())

        pair(i, column_tile)

        @pl.when(i == 2)
        def _():
            column_tile(z, 2)

        @pl.when(i == 3)
        def _():
            mate_copy(0).wait_recv()
            mate_copy(1).wait_recv()

        @pl.when(jnp.logical_and(s == 2, unit != 2))
        def _():
            local_tile(unit)

        @pl.when(i == 5)
        def _():
            finish(z, 2)
            shared_tile(z)

        @pl.when(i > 2)
        def _():
            pair(i - 3, finish)

        @pl.when(unit == 2)
        def _():
            for d in (0, 1):
                arrived(d, s, 3)

                @pl.when(s < 3)
                def _():
                    ring_copy(d, s, 3).start()

                @pl.when(s == 3)
                def _():
                    opposite(next_place[d], lambda up: ring_copy(d, s, 3, up).start())

            def one(d, carry):
                shared_tile(place_of(d, s))
                return carry

            lax.fori_loop(0, 2, one, 0)

        return carry

    lax.fori_loop(0, 9, visit, 0)

    far = lax.rem(z + 4, 8)

    def last(unit, carry):
        for d in (0, 1):
            opposite(z, lambda up: arrived(d, 4, unit, up))
        column_tile(far, unit)

        pair(6 + unit, finish)
        return carry

    lax.fori_loop(0, 3, last, 0)
    for d in (0, 1):
        opposite(z, lambda up: arrived(d, 4, 3, up))
    shared_tile(far)
    for unit in range(3):
        finish(far, unit)

    for unit in range(4):
        if unit != 2:
            mate_copy(unit).wait_send()
        for d in (0, 1):
            for s in range(3):
                ring_copy(d, s, unit).wait_send()
            opposite(next_place[d], lambda up: ring_copy(d, 3, unit, up).wait_send())

    def drain(i, carry):
        place = lax.rem(z + i, 8)
        for unit in range(3):
            sum_copy(place, unit, plain if unit == 2 else TILE).wait_send()
        return carry

    lax.fori_loop(1, 8, drain, 0)
    sum_copy(z, 2, plain).wait_send()
    pltpu.make_async_copy(peers, peers, spread_sem.at[0]).wait()
    swap.wait_send()

    @pl.when(z == 0)
    def _():
        ref = pieces.at[pl.ds(0, 7)]
        pltpu.make_async_copy(ref, ref, piece_sem.at[4]).wait()

    @pl.when(is_source)
    def _():
        ref = own.at[0, 0, pl.ds(0, 240)]
        pltpu.make_async_copy(ref, ref, piece_sem.at[0]).wait()

    @pl.when(is_couple)
    def _():
        ref = pieces.at[pl.ds(0, 2 * PIECE - 1), :, pl.ds(512, 128)]
        pltpu.make_async_copy(ref, ref, piece_sem.at[2]).wait()


def shards(panel_cols, inverses, trailing):
    bf16 = jnp.bfloat16
    return pl.pallas_call(
        kernel,
        out_shape=pltpu.VMEM(trailing.shape, bf16),
        in_specs=[
            pl.BlockSpec(memory_space=pl.ANY),
            pl.BlockSpec(memory_space=pltpu.VMEM),
            pl.BlockSpec(memory_space=pl.ANY),
        ],
        out_specs=pl.BlockSpec(memory_space=pltpu.VMEM),
        scratch_shapes=[
            pltpu.VMEM((8, 3, TILE, 2 * TILE), bf16),
            pltpu.VMEM((2, TILE, 2 * TILE), bf16),
            pltpu.VMEM((8, SHARED, 2 * TILE), bf16),
            pltpu.VMEM((8, 3, TILE, TILE), bf16),
            pltpu.VMEM((8, 3, TILE, TILE), bf16),
            pltpu.VMEM((8, 16, 640), bf16),
            pltpu.VMEM((16, 128), bf16),
            pltpu.VMEM((2 * PIECE, 16, 640), bf16),
            pltpu.VMEM((TILE, TILE), bf16),
            pltpu.VMEM((2, TILE, 2 * TILE), bf16),
            pltpu.SemaphoreType.DMA((2, 4, 4)),
            pltpu.SemaphoreType.DMA((2, 4, 4)),
            pltpu.SemaphoreType.DMA((4,)),
            pltpu.SemaphoreType.DMA((4,)),
            pltpu.SemaphoreType.DMA((8, 3)),
            pltpu.SemaphoreType.DMA((8, 3)),
            pltpu.SemaphoreType.DMA((2,)),
            pltpu.SemaphoreType.DMA((6,)),
            pltpu.SemaphoreType.DMA((4,)),
            pltpu.SemaphoreType.REGULAR((4,)),
        ],
        compiler_params=pltpu.CompilerParams(
            collective_id=0, has_side_effects=True, vmem_limit_bytes=56 << 20
        ),
        name="panel_update",
    )(panel_cols, inverses, trailing)


def solution(mesh):
    in_specs = (P("col", "row", None), P(), P(None, "row", "col"))
    out_specs = P(None, "row", "col")
    return jax.shard_map(shards, mesh=mesh, in_specs=in_specs, out_specs=out_specs, check_vma=False)
```

```python
import functools

import jax
import jax.numpy as jnp
from jax import lax
from jax.experimental import pallas as pl
from jax.experimental.pallas import tpu as pltpu
from jax.sharding import PartitionSpec as P

MESH = pl.DeviceIdType.MESH
TILE = 256
SHARED = 112
FIRST = 192
FEWER = 128
BEFORE = (3, 0)
PIECE = 16


def times_transposed(left, right):
    return lax.dot_general(left, right, (((1,), (1,)), ((), ())), preferred_element_type=jnp.float32)


def kernel(
    panel, inverses, trailing, window,
    own, mate, shared, sums_in, sums_out, stage, couple_piece, pieces, couple, keys,
    ring_send, ring_recv, mate_send, mate_recv, sum_send, sum_recv,
    load_sem, piece_sem, spread_sem, ready_sem,
):
    row, col = lax.axis_index("row"), lax.axis_index("col")
    z, y = col // 2, lax.rem(col, 2)
    chip, core = row // 2, lax.rem(row, 2)
    my_piece = core * PIECE + chip * 2 + y
    mate_dev = (row, col + 1 - 2 * y)
    core_dev = (row + 1 - 2 * core, col)
    ring_dev = ((row, lax.rem(col + 2, 16)), (row, lax.rem(col + 14, 16)))
    plain = TILE - SHARED

    load_own = pltpu.make_async_copy(panel, own.at[z], load_sem.at[0])
    load_window = pltpu.make_async_copy(trailing, window, load_sem.at[1])
    load_own.start()
    load_window.start()

    def plane_device(q, plane):
        at = lax.rem(q, PIECE)
        return ((at // 2) * 2 + q // PIECE, plane * 2 + lax.rem(at, 2))

    key_plane = lax.rem(row + 14, 16) // 2
    is_source = col == 0
    is_couple = jnp.logical_and(is_source, row == 1)

    barrier = pltpu.get_barrier_semaphore()

    def greet(dev):
        pl.semaphore_signal(barrier, inc=1, device_id=dev, device_id_type=MESH)

    @pl.when(z == 0)
    def _():
        def greet_place(place, carry):
            greet((row, place * 2 + y))
            return carry

        lax.fori_loop(1, 8, greet_place, 0)

    @pl.when(jnp.logical_and(z > 0, z < 6))
    def _():
        greet(ring_dev[0])

    @pl.when(z > 2)
    def _():
        greet(ring_dev[1])

    def greet_plane(p, carry):
        @pl.when(core * PIECE + p != my_piece)
        def _():
            greet(plane_device(core * PIECE + p, z))

        return carry

    lax.fori_loop(0, PIECE, greet_plane, 0)
    greet(core_dev)

    @pl.when(jnp.logical_and(jnp.logical_and(z == 0, core == 0), row + col > 0))
    def _():
        greet((1, 0))

    beside = jnp.logical_or(z == 1, z == 7)
    from_others = jnp.where(z == 0, 0, jnp.where(beside, 1, 3))
    pl.semaphore_wait(barrier, 16 + from_others + jnp.where(is_couple, 15, 0))

    @pl.when(z != 0)
    def _():
        pl.semaphore_signal(
            ready_sem.at[jnp.where(z == 1, 0, jnp.where(z == 7, 2, 1))], inc=1, device_id=(row, y), device_id_type=MESH
        )

    @pl.when(z == 2)
    def _():
        pl.semaphore_signal(ready_sem.at[3], inc=1, device_id=ring_dev[1], device_id_type=MESH)

    @pl.when(z == 6)
    def _():
        pl.semaphore_signal(ready_sem.at[3], inc=1, device_id=ring_dev[0], device_id_type=MESH)

    load_own.wait()

    def is_shared(unit):
        return isinstance(unit, int) and unit == 3

    def ring_ref(d, s, unit):
        place = lax.rem(z + 8 - s, 8) if d == 0 else lax.rem(z + s, 8)
        return shared.at[place] if is_shared(unit) else own.at[place, unit]

    def ring_copy(d, s, unit, up=None):
        ref = ring_ref(d, s, unit)
        if up is not None:
            rows = SHARED if is_shared(unit) else TILE
            up = up * rows // TILE // 16 * 16
            ref = ref.at[pl.ds(0, up)] if d == 0 else ref.at[pl.ds(up, rows - up)]
        return pltpu.make_async_remote_copy(
            ref, ref, ring_send.at[d, s, unit], ring_recv.at[d, s, unit],
            device_id=ring_dev[d], device_id_type=MESH,
        )

    def arrived(d, s, unit, up=None):
        ref = ring_ref(d, s, unit)
        if up is not None:
            rows = SHARED if is_shared(unit) else TILE
            up = up * rows // TILE // 16 * 16
            ref = ref.at[pl.ds(0, up)] if d == 0 else ref.at[pl.ds(up, rows - up)]
        pltpu.make_async_remote_copy(
            ref, ref, ring_send.at[d, s - 1, unit], ring_recv.at[d, s - 1, unit],
            device_id=ring_dev[d], device_id_type=MESH,
        ).wait_recv()

    def opposite(place, action):
        @pl.when(place == 1)
        def _():
            action(FEWER)

        @pl.when(place == 7)
        def _():
            action(TILE - FEWER)

        @pl.when(jnp.logical_and(place != 1, place != 7))
        def _():
            action(TILE // 2)

    next_place = (lax.rem(z + 1, 8), lax.rem(z + 7, 8))

    def mate_copy(unit):
        if unit == 3:
            ref, dst = own.at[z, 2, pl.ds(plain, SHARED)], shared.at[z]
        else:
            ref, dst = own.at[z, unit], mate.at[unit]
        return pltpu.make_async_remote_copy(
            ref, dst, mate_send.at[unit], mate_recv.at[unit], device_id=mate_dev, device_id_type=MESH
        )

    key_tile = jnp.where(row < 2, 1, 0)

    @pl.when(is_couple)
    def _():
        def send(q, carry):
            src = own.at[0, 0, pl.ds(lax.rem(q, PIECE) * 16, 16), pl.ds((q // PIECE) * 128, 128)]

            @pl.when(q != my_piece)
            def _():
                pltpu.make_async_remote_copy(
                    src, couple_piece, piece_sem.at[2], piece_sem.at[3], device_id=plane_device(q, 0),
                    device_id_type=MESH,
                ).start()

            @pl.when(q == my_piece)
            def _():
                pltpu.make_async_copy(src, couple_piece, piece_sem.at[3]).start()

            return carry

        lax.fori_loop(0, 2 * PIECE, send, 0)

    @pl.when(is_source)
    def _():
        def send(p, carry):
            q = core * PIECE + p
            src = own.at[0, key_tile, pl.ds(p * 16, 16)]
            dst = stage.at[key_plane, :, pl.ds(0, 512)]

            @pl.when(q != my_piece)
            def _():
                pltpu.make_async_remote_copy(
                    src, dst, piece_sem.at[0], piece_sem.at[1], device_id=plane_device(q, 0), device_id_type=MESH
                ).start()

            @pl.when(q == my_piece)
            def _():
                pltpu.make_async_copy(src, dst, piece_sem.at[1]).start()

            return carry

        lax.fori_loop(0, PIECE, send, 0)

    def begin(units, ways=(0, 1)):
        for unit in units:
            for d in ways:
                ring_copy(d, 0, unit).start()

    def begin_part(start, rows, ways=(0, 1)):
        if rows:
            for d in ways:
                ref = own.at[z, 0, pl.ds(start, rows)]
                pltpu.make_async_remote_copy(
                    ref, ref, ring_send.at[d, 0, 0], ring_recv.at[d, 0, 0], device_id=ring_dev[d], device_id_type=MESH
                ).start()

    mine = pieces.at[my_piece]

    def spread():
        def send(p, carry):
            q = core * PIECE + p

            @pl.when(q != my_piece)
            def _():
                pltpu.make_async_remote_copy(
                    mine, mine, spread_sem.at[0], spread_sem.at[1], device_id=plane_device(q, z), device_id_type=MESH
                ).start()

            return carry

        lax.fori_loop(0, PIECE, send, 0)
        for unit in (0, 1):
            if unit not in BEFORE:
                mate_copy(unit).start()

    def begin_mate():
        for unit in BEFORE:
            mate_copy(unit).start()

    @pl.when(z == 0)
    def _():
        begin_mate()
        pl.semaphore_wait(ready_sem.at[0], 1)
        begin_part(0, FIRST, (0,))
        pl.semaphore_wait(ready_sem.at[2], 1)
        begin_part(0, FIRST, (1,))
        staged = stage.at[:, :, pl.ds(0, 512)]
        pltpu.make_async_copy(couple_piece, couple_piece, piece_sem.at[3]).wait()
        pltpu.make_async_copy(staged, staged, piece_sem.at[1]).wait()
        for plane in range(8):
            stage[plane, :, 512:640] = couple_piece[...]
        pieces[my_piece] = stage[0]
        spread()
        pl.semaphore_wait(ready_sem.at[1], 5)

        def send(plane, carry):
            pltpu.make_async_remote_copy(
                stage.at[plane], mine, piece_sem.at[4], piece_sem.at[5], device_id=(row, plane * 2 + y),
                device_id_type=MESH,
            ).start()
            return carry

        lax.fori_loop(1, 8, send, 0)
        begin_part(FIRST, TILE - FIRST)
        begin((1, 2))

    def begin_beside(inward, outward):
        begin((0,), (inward,))
        begin_mate()
        begin((1, 2), (inward,))
        pl.semaphore_wait(ready_sem.at[3], 1)
        begin((0, 1, 2), (outward,))

    @pl.when(z == 1)
    def _():
        begin_beside(1, 0)

    @pl.when(z == 7)
    def _():
        begin_beside(0, 1)

    @pl.when(jnp.logical_and(z > 1, z < 7))
    def _():
        begin((0,))
        begin_mate()
        begin((1, 2))

    mate_copy(3).wait_recv()
    begin((3,))

    @pl.when(z != 0)
    def _():
        pltpu.make_async_copy(mine, mine, piece_sem.at[5]).wait()
        spread()

    peers = pieces.at[pl.ds(0, PIECE - 1)]
    half = pieces.at[pl.ds(core * PIECE, PIECE)]
    swap = pltpu.make_async_remote_copy(
        half, half, spread_sem.at[2], spread_sem.at[3], device_id=core_dev, device_id_type=MESH
    )

    for d in (0, 1):
        arrived(d, 1, 0)
        ring_copy(d, 1, 0).start()
    pltpu.make_async_copy(peers, peers, spread_sem.at[1]).wait()
    swap.start()
    for unit in (1, 2):
        for d in (0, 1):
            arrived(d, 1, unit)
            ring_copy(d, 1, unit).start()
    swap.wait_recv()

    for part in (0, 1):
        raw = pieces[part * PIECE:(part + 1) * PIECE, :, 512:640].reshape(TILE, 128)
        keys[0, :, part * 128:(part + 1) * 128] = raw
    couple[...] = times_transposed(keys[0, :, 0:TILE], inverses[0]).astype(jnp.bfloat16)

    def factor(raw):
        left = times_transposed(raw[:, 0:TILE], inverses[0]).astype(jnp.bfloat16)
        reduced = (raw[:, TILE:].astype(jnp.float32) - times_transposed(left, couple[...])).astype(jnp.bfloat16)
        right = times_transposed(reduced, inverses[1]).astype(jnp.bfloat16)
        return left, right

    def product(factors, which):
        left, right = factors
        return times_transposed(left, keys[which, :, 0:TILE]) + times_transposed(right, keys[which, :, TILE:])

    for which in (0, 1):
        parity = y if which == 0 else 1 - y
        raw = pieces[pl.ds(parity * PIECE, PIECE), :, 0:512].reshape(TILE, 2 * TILE)
        left, right = factor(raw)
        keys[which, :, 0:TILE] = left
        keys[which, :, TILE:] = right

    load_window.wait()

    def subtract(tile, start, rows, amount):
        at = (tile, pl.ds(start, rows))
        window[at] = (window[at].astype(jnp.float32) - amount.astype(jnp.float32)).astype(jnp.bfloat16)

    def own_tile(place, unit):
        return (place * 2 + y) * 3 + unit

    def mate_tile(place, unit):
        return (place * 2 + 1 - y) * 3 + unit

    def local_tile(unit):
        subtract(own_tile(z, unit), 0, TILE, product(factor(own[z, unit]), 0))
        subtract(mate_tile(z, unit), 0, TILE, product(factor(mate[unit]), 0))

    def place_of(d, s):
        return lax.rem(z + jnp.where(d == 0, 8 - s, s), 8)

    def sum_copy(place, unit, rows):
        return pltpu.make_async_remote_copy(
            sums_out.at[place, unit, pl.ds(0, rows)], sums_in.at[place, unit, pl.ds(0, rows)],
            sum_send.at[place, unit], sum_recv.at[place, unit], device_id=mate_dev, device_id_type=MESH,
        )

    def column_tile(place, unit):
        factors = factor(own[place, unit])
        sums_out[place, unit] = product(factors, 1).astype(jnp.bfloat16)

        @pl.when(unit != 2)
        def _():
            sum_copy(place, unit, TILE).start()

        @pl.when(unit == 2)
        def _():
            sum_copy(place, unit, plain).start()

        subtract(own_tile(place, unit), 0, TILE, product(factors, 0))

    def finish(place, unit):
        @pl.when(unit != 2)
        def _():
            sum_copy(place, unit, TILE).wait_recv()
            subtract(mate_tile(place, unit), 0, TILE, sums_in[place, unit])

        @pl.when(unit == 2)
        def _():
            sum_copy(place, unit, plain).wait_recv()
            subtract(mate_tile(place, unit), 0, plain, sums_in[place, unit, 0:plain])

    def shared_tile(place):
        subtract(mate_tile(place, 2), plain, SHARED, product(factor(shared[place]), 0))

    def pair(i, compute):
        s, unit = i // 3 + 1, lax.rem(i, 3)

        def one(d, carry):
            compute(place_of(d, s), unit)
            return carry

        lax.fori_loop(0, 2, one, 0)

    def visit(i, carry):
        s, unit = i // 3 + 1, lax.rem(i, 3)

        @pl.when(s > 1)
        def _():
            for d in (0, 1):
                arrived(d, s, unit)

                @pl.when(s == 2)
                def _():
                    ring_copy(d, s, unit).start()

                @pl.when(s == 3)
                def _():
                    opposite(next_place[d], lambda up: ring_copy(d, s, unit, up).start())

        pair(i, column_tile)

        @pl.when(i == 2)
        def _():
            column_tile(z, 2)

        @pl.when(i == 3)
        def _():
            mate_copy(0).wait_recv()
            mate_copy(1).wait_recv()

        @pl.when(jnp.logical_and(s == 2, unit != 2))
        def _():
            local_tile(unit)

        @pl.when(i == 5)
        def _():
            finish(z, 2)
            shared_tile(z)

        @pl.when(i > 2)
        def _():
            pair(i - 3, finish)

        @pl.when(unit == 2)
        def _():
            for d in (0, 1):
                arrived(d, s, 3)

                @pl.when(s < 3)
                def _():
                    ring_copy(d, s, 3).start()

                @pl.when(s == 3)
                def _():
                    opposite(next_place[d], lambda up: ring_copy(d, s, 3, up).start())

            def one(d, carry):
                shared_tile(place_of(d, s))
                return carry

            lax.fori_loop(0, 2, one, 0)

        return carry

    lax.fori_loop(0, 9, visit, 0)

    far = lax.rem(z + 4, 8)

    def last(unit, carry):
        for d in (0, 1):
            opposite(z, lambda up: arrived(d, 4, unit, up))
        column_tile(far, unit)

        pair(6 + unit, finish)
        return carry

    lax.fori_loop(0, 3, last, 0)
    for d in (0, 1):
        opposite(z, lambda up: arrived(d, 4, 3, up))
    shared_tile(far)
    for unit in range(3):
        finish(far, unit)

    for unit in range(4):
        if unit != 2:
            mate_copy(unit).wait_send()
        for d in (0, 1):
            for s in range(3):
                ring_copy(d, s, unit).wait_send()
            opposite(next_place[d], lambda up: ring_copy(d, 3, unit, up).wait_send())

    def drain(i, carry):
        place = lax.rem(z + i, 8)
        for unit in range(3):
            sum_copy(place, unit, plain if unit == 2 else TILE).wait_send()
        return carry

    lax.fori_loop(1, 8, drain, 0)
    sum_copy(z, 2, plain).wait_send()
    pltpu.make_async_copy(peers, peers, spread_sem.at[0]).wait()
    swap.wait_send()

    @pl.when(z == 0)
    def _():
        ref = pieces.at[pl.ds(0, 7)]
        pltpu.make_async_copy(ref, ref, piece_sem.at[4]).wait()

    @pl.when(is_source)
    def _():
        ref = own.at[0, 0, pl.ds(0, 240)]
        pltpu.make_async_copy(ref, ref, piece_sem.at[0]).wait()

    @pl.when(is_couple)
    def _():
        ref = pieces.at[pl.ds(0, 2 * PIECE - 1), :, pl.ds(512, 128)]
        pltpu.make_async_copy(ref, ref, piece_sem.at[2]).wait()


def shards(panel_cols, inverses, trailing):
    bf16 = jnp.bfloat16
    return pl.pallas_call(
        kernel,
        out_shape=pltpu.VMEM(trailing.shape, bf16),
        in_specs=[
            pl.BlockSpec(memory_space=pl.ANY),
            pl.BlockSpec(memory_space=pltpu.VMEM),
            pl.BlockSpec(memory_space=pl.ANY),
        ],
        out_specs=pl.BlockSpec(memory_space=pltpu.VMEM),
        scratch_shapes=[
            pltpu.VMEM((8, 3, TILE, 2 * TILE), bf16),
            pltpu.VMEM((2, TILE, 2 * TILE), bf16),
            pltpu.VMEM((8, SHARED, 2 * TILE), bf16),
            pltpu.VMEM((8, 3, TILE, TILE), bf16),
            pltpu.VMEM((8, 3, TILE, TILE), bf16),
            pltpu.VMEM((8, 16, 640), bf16),
            pltpu.VMEM((16, 128), bf16),
            pltpu.VMEM((2 * PIECE, 16, 640), bf16),
            pltpu.VMEM((TILE, TILE), bf16),
            pltpu.VMEM((2, TILE, 2 * TILE), bf16),
            pltpu.SemaphoreType.DMA((2, 4, 4)),
            pltpu.SemaphoreType.DMA((2, 4, 4)),
            pltpu.SemaphoreType.DMA((4,)),
            pltpu.SemaphoreType.DMA((4,)),
            pltpu.SemaphoreType.DMA((8, 3)),
            pltpu.SemaphoreType.DMA((8, 3)),
            pltpu.SemaphoreType.DMA((2,)),
            pltpu.SemaphoreType.DMA((6,)),
            pltpu.SemaphoreType.DMA((4,)),
            pltpu.SemaphoreType.REGULAR((4,)),
        ],
        compiler_params=pltpu.CompilerParams(
            collective_id=0, has_side_effects=True, vmem_limit_bytes=56 << 20
        ),
        name="panel_update",
    )(panel_cols, inverses, trailing)


def solution(mesh):
    in_specs = (P("col", "row", None), P(), P(None, "row", "col"))
    out_specs = P(None, "row", "col")
    return jax.shard_map(shards, mesh=mesh, in_specs=in_specs, out_specs=out_specs, check_vma=False)
```
